256 devices in a mesh: bx: 4 (over x), by: 32 (over y, z), gz: 2 (over core).
Axes of the slice: x: 4, y: 4, z: 8, core: 2. Of those that a mesh axis runs over, the one named last changes fastest.
Arguments:
- electric_start: float32 [3, 512, 64, 256], P(None, 'by', 'bx', 'gz'), may hold values from -6 to 6
- magnetic_start: float32 [3, 512, 64, 256], P(None, 'by', 'bx', 'gz'), may hold values from -6 to 6
- current_start: float32 [3, 512, 64, 256], P(None, 'by', 'bx', 'gz'), may hold values from -6 to 6
- cotangent: float32 [3, 512, 64, 256], P(None, 'by', 'bx', 'gz'), may hold values from -6 to 6
- level_set: float32 [512, 64, 256], P('by', 'bx', 'gz'), may hold values from -8 to 8
- material: int32 [512, 64, 256], P('by', 'bx', 'gz'), may hold values from 0 to 2
- source_cell: int32 [2048], P(('bx', 'by', 'gz')), may hold values from 0 to 32767
- basis: bfloat16 [65536, 64, 256], P(('bx', 'by', 'gz')), may hold values from 0 to 1
- block_owner: int32 [65536, 1], P(('bx', 'by', 'gz')), may hold values from 0 to 127; in each aligned block of 256 rows (0 to 255, 256 to 511, ...) at most 4 rows name the same one
- block_group: int32 [65536], P(('bx', 'by', 'gz')), may hold values from 0 to 127
Outputs:
- final_electric: float32 [3, 512, 64, 256], P(None, 'by', 'bx', 'gz')
- adjoint_electric: float32 [3, 512, 64, 256], P(None, 'by', 'bx', 'gz')
- coef_grad: float32 [64, 32768], P(None, ('bx', 'by', 'gz'))
The draws below stay inside these ranges and needn't reach their ends.
Inputs may be any that keep to these rules, and one draw needn't show every extreme that they name: `material`: 0 is vacuum, 1 design dielectric, 2 silver. `source_cell`: a flat cell index within the device's own brick; a cell may be named more than once. `block_owner`: among the 256 blocks of one device no owner is named by more than 4 blocks, and in some device one owner is named by exactly 4.
All inputs are finite; a program needn't handle non-finite values.
Results may differ from the reference program's by a relative error of at most 0.0029.
Values sent between devices are 32-bit elements; how exact they have to be, the bound alone decides.
A program may use at most 64 MiB of HBM per device.

```python
import math
import jax
import jax.numpy as jnp
import numpy as np
from jax import lax

CY = 16
CX = 16
CZ = 128
NSTEP = 2
KB = 64
TILE = 256
FAN = 2
GRP_DEV = 128
SRC_DEV = 8
NX = 64
NY = 512
NZ = 256
CELLS = 32768
TILES = 128
NB = 256
PLANES = 128
CAP = 4
GROUPS = 32768
N_BX = 4
N_BY = 32
N_GZ = 2


def place_ends(array, own_key, low, high):
    extent = array.shape
    spot = [jax.random.randint(jax.random.fold_in(own_key, axis), (), 0, extent[axis]) for axis in range(len(extent))]
    array = array.at[tuple(spot)].set(low)
    longest = extent.index(max(extent))
    spot[longest] = (spot[longest] + 1) % extent[longest]
    return array.at[tuple(spot)].set(high)


def level_of(rng, shape, shards, low, largest):
    level, own = 1.0, jax.random.fold_in(rng, 6)
    for position, blocks in shards:
        steps = jnp.exp(jax.random.uniform(jax.random.fold_in(own, position), (blocks,), jnp.float32, low / len(shards), largest / len(shards)))
        level = level * jnp.repeat(steps, shape[position] // blocks).reshape([-1 if axis == position else 1 for axis in range(len(shape))])
    return level


def deal_out(key, own, number, rows, count, top, limit, skew):
    sequence = jax.random.permutation(key, count)
    packed, ordinary = shares(count, rows * top, limit, skew, True), shares(count, rows * top, limit, skew, False)
    places = jnp.arange(count)

    def named(lengths, offset_by):
        used = int((lengths > 0).sum())
        fixed = max(1, used // 4)
        passed = fixed + (places - fixed + offset_by * (used - fixed)) % max(1, count - fixed)
        return jnp.zeros((count,), jnp.int32).at[sequence[jnp.where(places < fixed, places, passed)]].set(jnp.asarray(lengths, jnp.int32))

    lengths = jnp.where(number % 4 == 0, named(packed, number // 4), named(ordinary, number - number // 4 - 1))
    mixed = jax.random.permutation(jax.random.fold_in(own, 3), count)
    source_of, receiver = mixed[0:count // 2 * 2:2], mixed[1:count // 2 * 2:2]
    room = jnp.minimum(lengths[source_of] - 1, limit - lengths[receiver]) // 2
    room = jnp.where((source_of == sequence[0]) | (receiver == sequence[0]) | (lengths[receiver] == 0), 0, jnp.maximum(room, 0))
    passed = jax.random.randint(jax.random.fold_in(own, 4), (count // 2,), 0, 1 << 20) % (room + 1)
    lengths = lengths.at[source_of].add(-passed).at[receiver].add(passed)
    members = jnp.searchsorted(jnp.cumsum(lengths), jnp.arange(rows * top), side="right").astype(jnp.int32)
    listing = members.reshape(top, rows).T
    listing = listing[jax.random.permutation(jax.random.fold_in(own, 1), rows)]
    offset_by = jax.random.randint(jax.random.fold_in(own, 2), (rows, 1), 0, top)
    return jnp.take_along_axis(listing, (jnp.arange(top)[None, :] + offset_by) % top, axis=1)


def shares(amount, total, most, slope, full):
    weights = [(1 << 20) // math.isqrt(standing ** slope) + 1 for standing in range(1, amount + 1)]
    largest = most if full else min(most, max(-(-total // amount), total * weights[0] // sum(weights)))
    least = 1 if total - largest >= amount - 1 else 0
    holding, spare = [largest] + [least] * (amount - 1), total - largest - least * (amount - 1)
    while spare > 0:
        movable = [i for i in range(1, amount) if holding[i] < largest] or [i for i in range(1, amount) if holding[i] < most]
        mass, remaining = sum([weights[i] for i in movable]), spare
        for i in movable:
            extra = min(most - holding[i], max(1, remaining * weights[i] // mass), spare)
            holding[i] = holding[i] + extra
            spare = spare - extra
    return np.array(holding)


def bell_draw(own_key, shape, scale, most, cuts=(), held_as=jnp.bfloat16):
    gain = level_of(own_key, shape, cuts, -0.22, 0.18) if cuts else 1.0
    result = jax.random.normal(own_key, shape, jnp.float32) * scale * gain
    return jnp.minimum(jnp.maximum(result, -most), most).astype(held_as)


def setup_inputs(seed: int = 0) -> dict:
    splits = jax.random.split(jax.random.key(seed), 11)
    electric_start = bell_draw(splits[0], (3, NY, NX, NZ), 1.0, 6.0, ((1, 32), (2, 4), (3, 2)), jnp.float32)
    magnetic_start = bell_draw(splits[1], (3, NY, NX, NZ), 1.0, 6.0, ((1, 32), (2, 4), (3, 2)), jnp.float32)
    current_start = bell_draw(splits[2], (3, NY, NX, NZ), 1.0, 6.0, ((1, 32), (2, 4), (3, 2)), jnp.float32)
    cotangent = bell_draw(splits[3], (3, NY, NX, NZ), 1.0, 6.0, ((1, 32), (2, 4), (3, 2)), jnp.float32)
    level_set = bell_draw(splits[4], (NY, NX, NZ), 2.0, 8.0, ((0, 32), (1, 4), (2, 2)), jnp.float32)
    material = place_ends(jax.random.randint(splits[5], (NY, NX, NZ), 0, 3), jax.random.fold_in(splits[5], 1), 0, 2).astype(jnp.int32)
    source_cell = place_ends(jax.random.randint(splits[6], (SRC_DEV * N_BX * N_BY * N_GZ,), 0, CELLS), jax.random.fold_in(splits[6], 1), 0, CELLS - 1).astype(jnp.int32)
    basis = jnp.clip(1.0 * jax.random.uniform(splits[7], (NB * N_BX * N_BY * N_GZ, KB, TILE), jnp.float32) ** level_of(splits[7], (NB * N_BX * N_BY * N_GZ, KB, TILE), ((0, 256),), -0.2, 0.2), 0.0, 1.0).astype(jnp.bfloat16)
    block_owner_keys = jax.random.split(jax.random.fold_in(splits[8], 1), (NB * N_BX * N_BY * N_GZ) // NB)
    block_owner_turns = jax.random.permutation(jax.random.fold_in(splits[8], 3), (NB * N_BX * N_BY * N_GZ) // NB)
    block_owner = jax.vmap(lambda own, number: deal_out(jax.random.fold_in(splits[8], 2), own, number, NB, PLANES, 1, CAP, 2))(block_owner_keys, block_owner_turns).reshape((NB * N_BX * N_BY * N_GZ, 1))
    block_group = place_ends(jax.random.randint(splits[9], (NB * N_BX * N_BY * N_GZ,), 0, GRP_DEV), jax.random.fold_in(splits[9], 1), 0, GRP_DEV - 1).astype(jnp.int32)
    return {"electric_start": electric_start, "magnetic_start": magnetic_start, "current_start": current_start, "cotangent": cotangent, "level_set": level_set, "material": material, "source_cell": source_cell, "basis": basis, "block_owner": block_owner, "block_group": block_group}


time_step = 0.5
drude_keep = 0.9
drude_gain = 1.0
metal_permit = 3.0
design_contrast = 5.0
source_level = 3.0
source_wave = (1.0, -0.6, 0.8, -0.4)

def beside(couple, axis_dim, offset):
    length = couple.shape[axis_dim]
    border = jnp.zeros_like(lax.slice_in_dim(couple, 0, 1, axis=axis_dim))
    if offset < 0:
        return jnp.concatenate([lax.slice_in_dim(couple, 1, length, axis=axis_dim), border], axis=axis_dim)
    return jnp.concatenate([border, lax.slice_in_dim(couple, 0, length - 1, axis=axis_dim)], axis=axis_dim)

def differ(couple, axis_dim, offset):
    neighbour = beside(couple, axis_dim, offset)
    if offset < 0:
        return neighbour - couple
    return couple - neighbour

def curl(fields, offset):
    along_x = differ(jnp.stack([fields[1], fields[2]]), 2, offset)
    along_y = differ(jnp.stack([fields[0], fields[2]]), 1, offset)
    along_z = differ(jnp.stack([fields[0], fields[1]]), 3, offset)
    return jnp.stack([along_y[1] - along_z[1], along_z[0] - along_x[1], along_x[0] - along_y[0]])

def permittivity(material, level_set):
    smooth = jax.nn.sigmoid(level_set)
    return jnp.where(material == 2, metal_permit, jnp.where(material == 1, 1.0 + design_contrast * smooth, 1.0))

def forward(electric, magnetic, current, permit, silver, sources):
    for moment in range(NSTEP):
        magnetic = magnetic - time_step * curl(electric, -1)
        current = silver * (drude_keep * current + drude_gain * electric)
        drive_term = curl(magnetic, 1) - current
        electric = electric + time_step / permit * drive_term
        electric = electric.at[2].add(source_level * source_wave[moment] * sources)
    return electric

def reference(electric_start, magnetic_start, current_start, cotangent, level_set, material, source_cell, basis, block_owner, block_group):
    silver = (material == 2).astype(jnp.float32)
    devices = N_BX * N_BY * N_GZ
    src_rows = jnp.arange(SRC_DEV * devices, dtype=jnp.int32)
    src_dev = src_rows // SRC_DEV
    dev_bx = src_dev // (N_BY * N_GZ)
    dev_by = src_dev // N_GZ % N_BY
    dev_gz = src_dev % N_GZ
    local_y = source_cell // (CX * CZ)
    local_x = source_cell // CZ % CX
    local_z = source_cell % CZ
    sources = jnp.zeros((NY, NX, NZ), jnp.float32).at[dev_by * CY + local_y, dev_bx * CX + local_x, dev_gz * CZ + local_z].add(1.0)

    def propagate(start_field, level_field):
        return forward(start_field, magnetic_start, current_start, permittivity(material, level_field), silver, sources)
    final_field, pullback = jax.vjp(propagate, electric_start, level_set)
    adjoint, level_grad = pullback(cotangent)
    cell_grad = level_grad.astype(jnp.bfloat16)
    bricks = cell_grad.reshape(N_BY, CY, N_BX, CX, N_GZ, CZ).transpose(2, 0, 4, 1, 3, 5).reshape(devices, TILES, TILE)
    blocks = basis.reshape(devices, TILES, FAN, KB, TILE)

    def project(couple):
        return jnp.einsum('tfkc,tc->tfk', couple[0].astype(jnp.float32), couple[1].astype(jnp.float32))
    partials = lax.map(project, (blocks, bricks)).reshape(devices * NB, KB)
    block_rows = jnp.arange(devices * NB, dtype=jnp.int32)
    plane_gz = block_rows // NB % N_GZ
    group_index = (block_owner[:, 0] * N_GZ + plane_gz) * GRP_DEV + block_group
    coef_sum = jax.ops.segment_sum(partials, group_index, num_segments=GROUPS)
    return (final_field, adjoint, coef_sum.T)
```

```python
import jax
import jax.numpy as jnp
from jax import lax
from jax.experimental import pallas as pl
from jax.experimental.pallas import tpu as pltpu
from jax.sharding import PartitionSpec as P

KB = 64
GRP_DEV = 128
NBX = 4
NBY = 32
PLANES = 128
NB = 256
TILES = 128
TILE = 256
NCHUNK = 8

time_step = 0.5
drude_keep = 0.9
drude_gain = 1.0
metal_permit = 3.0
design_contrast = 5.0
source_level = 3.0
source_wave = (1.0, -0.6, 0.8, -0.4)

F32 = jnp.float32
BF16 = jnp.bfloat16
MESH = pl.DeviceIdType.MESH

IDX = {("x", 0): 0, ("z", 0): 1, ("x", 1): 2, ("z", 1): 3, ("y", 0): 4, ("y", 1): 5}
COMP = {"x": 0, "y": 1, "z": 2}


def iota(shape, dim):
    return lax.broadcasted_iota(jnp.int32, shape, dim)


def split(v):
    hi = v.astype(BF16)
    lo = (v - hi.astype(F32)).astype(BF16)
    return hi, lo


def kernel(
    source_ref,
    e0_hbm,
    h0_hbm,
    j0_hbm,
    cot_hbm,
    level_hbm,
    material_hbm,
    basis_hbm,
    owner_hbm,
    group_hbm,
    e_out,
    a_out,
    coef_out,
    p1,
    p2,
    m1,
    m2,
    h0,
    j0,
    cot,
    level,
    material,
    ratio,
    silver,
    factor,
    sources,
    d1,
    adj1,
    part1,
    grad,
    efin,
    afin,
    basis,
    owner,
    group,
    xsend,
    xrecv,
    zsend,
    zrecv,
    place,
    partial,
    vsend,
    vrecv,
    isend,
    irecv,
    coef,
    in_sem,
    basis_sem,
    out_sem,
    send_sem,
    recv_sem,
    a2a_sem,
    own_sem,
    ready_sem,
):
    bx, by, gz = lax.axis_index("bx"), lax.axis_index("by"), lax.axis_index("gz")
    me = bx * NBY + by
    yy, zz = by // 8, by % 8
    xy = bx * 4 + yy

    loads = [
        (material_hbm, material),
        (level_hbm, level),
        (cot_hbm, cot),
        (e0_hbm.at[0], p1.at[0, pl.ds(0, 16)]),
        (e0_hbm.at[2], p1.at[1, pl.ds(0, 16)]),
        (e0_hbm.at[1], p1.at[4, pl.ds(0, 16)]),
        (h0_hbm, h0),
        (j0_hbm, j0),
        (owner_hbm, owner),
        (group_hbm, group),
    ]
    loads = [pltpu.make_async_copy(s, d, in_sem.at[i]) for i, (s, d) in enumerate(loads)]
    for c in loads:
        c.start()

    zrow = jnp.zeros((4, 16, 128), F32)
    for ref, at in ((p1, 16), (p2, 16), (m1, 0), (m2, 0)):
        ref[0:4, at] = zrow
    for r in range(4):
        xrecv[r] = zrow
        zrecv[r] = jnp.zeros((16, 128), F32)

    barrier = pltpu.get_barrier_semaphore()

    def hail(**where):
        pl.semaphore_signal(barrier, inc=1, device_id=where, device_id_type=MESH)

    for i in range(1, 8):
        hail(by=yy * 8 + (zz + i) % 8)
    for i in range(1, 16):
        q = (xy + i) % 16
        hail(bx=q // 4, by=(q % 4) * 8 + zz)
    hail(gz=1 - gz)
    up_far = jnp.logical_and(zz == 7, by < NBY - 1)
    down_far = jnp.logical_and(zz == 0, by > 0)

    @pl.when(up_far)
    def _():
        hail(by=by + 1)

    @pl.when(down_far)
    def _():
        hail(by=by - 1)

    for c in loads[:6]:
        c.wait()
    bases = [
        pltpu.make_async_copy(
            basis_hbm.at[pl.ds(i * (NB * KB // NCHUNK), NB * KB // NCHUNK)],
            basis.at[pl.ds(i * (NB * KB // NCHUNK), NB * KB // NCHUNK)],
            basis_sem.at[i],
        )
        for i in range(NCHUNK)
    ]
    for c in bases:
        c.start()

    row = iota((16, 128), 0)
    lane = iota((16, 128), 1)

    def pack_z(acc, y, vals, from_lane):
        for c, v in enumerate(vals):
            at = 4 * y + c
            acc = jnp.where(lane == at, pltpu.roll(v, (at + 128 - from_lane) % 128, 1), acc)
        return acc

    def first(y, acc):
        mat = material[y]
        lev = level[y]
        smooth = jax.nn.sigmoid(lev)
        design = (mat == 1).astype(F32)
        sil = (mat == 2).astype(F32)
        permit = jnp.where(mat == 2, metal_permit, jnp.where(mat == 1, 1.0 + design_contrast * smooth, 1.0))
        rat = time_step / permit
        ratio[y] = rat
        silver[y] = sil
        factor[y] = -(design * design_contrast * (smooth * (1.0 - smooth))) / permit
        sx, sy, sz = (rat * cot[c, y] for c in range(3))
        p1[2, y] = sx
        p1[3, y] = sz
        p1[5, y] = sy
        ex, ey, ez = p1[0, y], p1[4, y], p1[1, y]
        for c, v in enumerate((ey, ez, sy, sz)):
            xsend[0, c, pl.ds(y, 1), :] = v[0:1]
        return pack_z(acc, y, (ex, ey, sx, sy), 0)

    zsend[0] = lax.fori_loop(0, 16, first, jnp.zeros((16, 128), F32))

    pl.semaphore_wait(barrier, 23 + up_far.astype(jnp.int32) + down_far.astype(jnp.int32))
    for i in range(1, 16):
        q = (xy + i) % 16
        pl.semaphore_signal(
            ready_sem, inc=1, device_id={"bx": q // 4, "by": (q % 4) * 8 + zz}, device_id_type=MESH
        )

    def moves(r, field):
        plus = r % 2 == 0
        step = -1 if plus else 1
        edge, halo = (0, 16) if plus else (16, 0)

        def move(src, dst, i, **where):
            return pltpu.make_async_remote_copy(
                src_ref=src,
                dst_ref=dst,
                send_sem=send_sem.at[r, i],
                recv_sem=recv_sem.at[r, i],
                device_id=where,
                device_id_type=MESH,
            )

        y_out = by > 0 if plus else by < NBY - 1
        y_in = by < NBY - 1 if plus else by > 0
        x_out = bx > 0 if plus else bx < NBX - 1
        x_in = bx < NBX - 1 if plus else bx > 0
        z_out = gz == 1 if plus else gz == 0
        z_in = gz == 0 if plus else gz == 1
        return (
            (y_out, y_in, move(field.at[pl.ds(0, 4), edge], field.at[pl.ds(0, 4), halo], 0, by=by + step)),
            (x_out, x_in, move(xsend.at[r], xrecv.at[r], 1, bx=bx + step)),
            (z_out, z_in, move(zsend.at[r], zrecv.at[r], 2, gz=1 - gz)),
        )

    def send(r, field):
        for out, _, c in moves(r, field):
            pl.when(out)(c.start)

    def receive(r, field):
        for out, into, c in moves(r, field):
            pl.when(into)(c.wait_recv)
            pl.when(out)(c.wait_send)

    send(0, p1)

    for c in loads[6:]:
        c.wait()

    def count(y, _):
        flat = y * 2048 + row * 128 + lane
        total = jnp.zeros((16, 128), F32)
        for i in range(8):
            total = total + (flat == source_ref[i]).astype(F32)
        sources[y] = total
        return 0

    lax.fori_loop(0, 16, count, 0)

    owner_row = owner[...].astype(F32)
    group_row = group[...].astype(F32)
    ri, ci = iota((NB, NB), 0), iota((NB, NB), 1)
    owner_wide = jnp.broadcast_to(owner_row, (NB, NB))
    owner_col = jnp.sum(jnp.where(ri == ci, owner_wide, 0.0), axis=1, keepdims=True)
    group_col = jnp.sum(jnp.where(ri == ci, jnp.broadcast_to(group_row, (NB, NB)), 0.0), axis=1, keepdims=True)
    same = jnp.logical_and(owner_wide == owner_col, ci < ri)
    rank_col = jnp.sum(same.astype(F32), axis=1, keepdims=True)
    target_col = owner_col * 4.0 + rank_col
    block, tile = iota((NB, TILES), 0), iota((NB, TILES), 1)
    id_sum = jnp.zeros((PLANES, 128), F32)
    dest, id_lane = iota((PLANES, TILES), 0), iota((PLANES, TILES), 1)
    targets, groups = [], []
    for f in range(2):
        pick = block == 2 * tile + f
        targets.append(jnp.sum(jnp.where(pick, target_col, 0.0), axis=0, keepdims=True))
        groups.append(jnp.sum(jnp.where(pick, group_col, 0.0), axis=0, keepdims=True))
    slot_row = (2 * iota((NB, TILES), 0)).astype(F32)
    for h in range(2):
        for f in range(2):
            place[:, pl.ds((2 * h + f) * TILES, TILES)] = (
                (targets[f] == slot_row + float(h)).astype(F32).astype(BF16)
            )
    first_slot = (4 * dest).astype(F32)
    for s in range(4):
        hit = jnp.zeros((PLANES, TILES), F32)
        for f in range(2):
            hit = hit + jnp.where(targets[f] == first_slot + float(s), groups[f], 0.0)
        id_sum = jnp.where(id_lane == s, jnp.sum(hit, axis=1, keepdims=True), id_sum)
    isend[:, 0, :] = id_sum

    def plus_half(r, field, old, out):
        nxt = r + 1

        def body(y, acc):
            zf = zrecv[r]
            vals = {}
            for s in range(2):
                fx, fy, fz = (field[IDX[(c, s)], y] for c in "xyz")
                dyx = field[IDX[("x", s)], y + 1] - fx
                dyz = field[IDX[("z", s)], y + 1] - fz

                def along_x(v, c):
                    return jnp.where(row == 15, xrecv[r, c, pl.ds(y, 1), :], pltpu.roll(v, 15, 0)) - v

                def along_z(v, c):
                    return jnp.where(lane == 127, pltpu.roll(zf, 127 - 4 * y - c, 1), pltpu.roll(v, 127, 1)) - v

                dxy, dxz = along_x(fy, 2 * s), along_x(fz, 2 * s + 1)
                dzx, dzy = along_z(fx, 2 * s), along_z(fy, 2 * s + 1)
                turn = {"x": dyz - dzy, "y": dzx - dxz, "z": dxy - dyx}
                for c in "xyz":
                    new = old(s, c, y, turn[c])
                    out[IDX[(c, s)], y + 1] = new
                    vals[(c, s)] = new
            for i, k in enumerate((("y", 0), ("z", 0), ("y", 1), ("z", 1))):
                xsend[nxt, i, pl.ds(y, 1), :] = vals[k][15:16]
            return pack_z(acc, y, [vals[k] for k in (("x", 0), ("y", 0), ("x", 1), ("y", 1))], 127)

        zsend[nxt] = lax.fori_loop(0, 16, body, jnp.zeros((16, 128), F32))

    def minus_turn(r, field, y, s):
        zf = zrecv[r]
        fx, fy, fz = (field[IDX[(c, s)], y + 1] for c in "xyz")
        dyx = fx - field[IDX[("x", s)], y]
        dyz = fz - field[IDX[("z", s)], y]

        def along_x(v, c):
            return v - jnp.where(row == 0, xrecv[r, c, pl.ds(y, 1), :], pltpu.roll(v, 1, 0))

        def along_z(v, c):
            return v - jnp.where(lane == 0, pltpu.roll(zf, 128 - 4 * y - c, 1), pltpu.roll(v, 1, 1))

        dxy, dxz = along_x(fy, 2 * s), along_x(fz, 2 * s + 1)
        dzx, dzy = along_z(fx, 2 * s), along_z(fy, 2 * s + 1)
        return {"x": dyz - dzy, "y": dzx - dxz, "z": dxy - dyx}

    def old_first(s, c, y, turn):
        return turn if s else h0[COMP[c], y] - time_step * turn

    def old_second(s, c, y, turn):
        before = m1[IDX[(c, s)], y + 1]
        return before + turn if s else before - time_step * turn

    receive(0, p1)
    plus_half(0, p1, old_first, m1)
    send(1, m1)

    pl.semaphore_wait(ready_sem, 15)

    def spread(src, dst, width, k):
        def one(i, _):
            p = (me + i) % PLANES
            pltpu.make_async_remote_copy(
                src_ref=src.at[pl.ds(p * width, width)],
                dst_ref=dst.at[pl.ds(me * width, width)],
                send_sem=a2a_sem.at[k, 0],
                recv_sem=a2a_sem.at[k, 1],
                device_id={"bx": p // NBY, "by": p % NBY},
                device_id_type=MESH,
            ).start()
            return 0

        own = pltpu.make_async_copy(
            src.at[pl.ds(me * width, width)], dst.at[pl.ds(me * width, width)], own_sem.at[k]
        )
        own.start()
        lax.fori_loop(1, PLANES, one, 0, unroll=4)

    def gathered(src, dst, width, k):
        many = pl.ds(0, (PLANES - 1) * width)
        pltpu.make_async_copy(src.at[many], src.at[many], a2a_sem.at[k, 0]).wait()
        pltpu.make_async_copy(dst.at[many], dst.at[many], a2a_sem.at[k, 1]).wait()
        pltpu.make_async_copy(
            src.at[pl.ds(me * width, width)], dst.at[pl.ds(me * width, width)], own_sem.at[k]
        ).wait()

    spread(isend, irecv, 1, 0)

    receive(1, m1)

    def electric_first(y, acc):
        rat, sil = ratio[y], silver[y]
        turn, back = minus_turn(1, m1, y, 0), minus_turn(1, m1, y, 1)
        total = jnp.zeros((16, 128), F32)
        fwd, adj = {}, {}
        for c in "xyz":
            e = p1[IDX[(c, 0)], y]
            cur = sil * (drude_keep * j0[COMP[c], y] + drude_gain * e)
            drive = turn[c] - cur
            j0[COMP[c], y] = cur
            new = e + rat * drive
            if c == "z":
                new = new + source_level * source_wave[0] * sources[y]
            fwd[c] = new
            p2[IDX[(c, 0)], y] = new
            scaled = p1[IDX[(c, 1)], y]
            a = cot[COMP[c], y] - drude_gain * (sil * scaled) - time_step * back[c]
            adj1[COMP[c], y] = a
            s0 = rat * a
            adj[c] = s0
            p2[IDX[(c, 1)], y] = s0
            total = total + s0 * drive
        part1[y] = total
        for i, v in enumerate((fwd["y"], fwd["z"], adj["y"], adj["z"])):
            xsend[2, i, pl.ds(y, 1), :] = v[0:1]
        return pack_z(acc, y, (fwd["x"], fwd["y"], adj["x"], adj["y"]), 0)

    zsend[2] = lax.fori_loop(0, 16, electric_first, jnp.zeros((16, 128), F32))
    send(2, p2)
    receive(2, p2)
    plus_half(2, p2, old_second, m2)
    send(3, m2)
    receive(3, m2)

    def electric_second(y, _):
        rat, sil = ratio[y], silver[y]
        turn, back = minus_turn(3, m2, y, 0), minus_turn(3, m2, y, 1)
        total = part1[y]
        for c in "xyz":
            e = p2[IDX[(c, 0)], y]
            cur = sil * (drude_keep * j0[COMP[c], y] + drude_gain * e)
            drive = turn[c] - cur
            new = e + rat * drive
            if c == "z":
                new = new + source_level * source_wave[1] * sources[y]
            efin[COMP[c], y] = new
            scaled = p1[IDX[(c, 1)], y]
            s0 = p2[IDX[(c, 1)], y]
            adj_drive = -drude_keep * (sil * scaled) - s0
            afin[COMP[c], y] = adj1[COMP[c], y] + drude_gain * (sil * adj_drive) - time_step * back[c]
            total = total + scaled * drive
        grad[pl.ds(pl.multiple_of(y * 16, 16), 16), :] = factor[y] * total
        return 0

    lax.fori_loop(0, 16, electric_second, 0)
    outs = [
        pltpu.make_async_copy(efin, e_out, out_sem.at[0]),
        pltpu.make_async_copy(afin, a_out, out_sem.at[1]),
    ]
    for c in outs:
        c.start()
    for c in bases:
        c.wait()

    low128 = iota((16, 128), 1) < 64
    r256, l256 = iota((16, 256), 0), iota((16, 256), 1)

    def tiles(i, _):
        start = pl.multiple_of(i * 16, 16)
        even = grad[pl.ds(2 * start, 16, stride=2), :]
        odd = grad[pl.ds(2 * start + 1, 16, stride=2), :]
        lhs = jnp.concatenate([even.astype(BF16), odd.astype(BF16)], axis=1)
        acc = jnp.zeros((16, 256), F32)
        for j in range(8):
            w = basis[pl.ds(pl.multiple_of(i * 2048 + j * 256, 256), 256), :]
            got = lax.dot_general(lhs, w, (((1,), (1,)), ((), ())), preferred_element_type=F32)
            acc = jnp.where(r256 == 2 * j + l256 // 128, got, acc)
        partial[pl.ds(start, 16), :] = jnp.where(row % 2 == 0, acc[:, :128], acc[:, 128:])
        return 0

    lax.fori_loop(0, 8, tiles, 0)

    part = partial[...]
    turned = pltpu.roll(part, 64, 1)
    low = iota((TILES, 128), 1) < 64
    stack = jnp.concatenate(
        [
            jnp.where(low, part, 0.0),
            jnp.where(low, turned, 0.0),
            jnp.where(low, 0.0, turned),
            jnp.where(low, 0.0, part),
        ],
        axis=0,
    )
    hi, lo = split(stack)
    slots = lax.dot_general(place[...], hi, (((1,), (0,)), ((), ())), preferred_element_type=F32)
    slots = slots + lax.dot_general(place[...], lo, (((1,), (0,)), ((), ())), preferred_element_type=F32)
    vsend[:, 0, :] = slots
    spread(vsend, vrecv, 2, 1)

    gathered(isend, irecv, 1, 0)
    ids = irecv[:, 0, :]
    group_lane = iota((PLANES, GRP_DEV), 1).astype(F32)
    hits = jnp.concatenate(
        [
            jnp.concatenate(
                [(ids[:, 2 * p + h : 2 * p + h + 1] == group_lane).astype(F32).astype(BF16) for h in range(2)], axis=1
            )
            for p in range(2)
        ],
        axis=0,
    )
    gathered(vsend, vrecv, 2, 1)
    vals = jnp.concatenate([vrecv[pl.ds(p, PLANES, stride=2), 0, :] for p in range(2)], axis=0)
    hi, lo = split(vals)
    both = lax.dot_general(hi, hits, (((0,), (0,)), ((), ())), preferred_element_type=F32)
    both = both + lax.dot_general(lo, hits, (((0,), (0,)), ((), ())), preferred_element_type=F32)
    coef[...] = both[:KB, :GRP_DEV] + both[KB:, GRP_DEV:]
    last = pltpu.make_async_copy(coef, coef_out, out_sem.at[2])
    last.start()
    for c in outs:
        c.wait()
    last.wait()


def local(
    electric_start,
    magnetic_start,
    current_start,
    cotangent,
    level_set,
    material,
    source_cell,
    basis,
    block_owner,
    block_group,
):
    field = (3, 16, 16, 128)
    brick = (16, 16, 128)
    anywhere = pl.BlockSpec(memory_space=pl.ANY)
    V, D = pltpu.VMEM, pltpu.SemaphoreType.DMA
    return pl.pallas_call(
        kernel,
        name="adjoint_step",
        out_shape=(
            jax.ShapeDtypeStruct(field, F32),
            jax.ShapeDtypeStruct(field, F32),
            jax.ShapeDtypeStruct((KB, GRP_DEV), F32),
        ),
        in_specs=[pl.BlockSpec(memory_space=pltpu.SMEM)] + [anywhere] * 9,
        out_specs=(anywhere,) * 3,
        scratch_shapes=[
            V((6, 17, 16, 128), F32),
            V((6, 17, 16, 128), F32),
            V((6, 17, 16, 128), F32),
            V((6, 17, 16, 128), F32),
            V(field, F32),
            V(field, F32),
            V(field, F32),
            V(brick, F32),
            V(brick, jnp.int32),
            V(brick, F32),
            V(brick, F32),
            V(brick, F32),
            V(brick, F32),
            V((8, 128), F32),
            V(field, F32),
            V(brick, F32),
            V((256, 128), F32),
            V(field, F32),
            V(field, F32),
            V((NB * KB, TILE), BF16),
            V((1, NB), jnp.int32),
            V((1, NB), jnp.int32),
            V((4, 4, 16, 128), F32),
            V((4, 4, 16, 128), F32),
            V((4, 16, 128), F32),
            V((4, 16, 128), F32),
            V((NB, 4 * TILES), BF16),
            V((TILES, 128), F32),
            V((NB, 1, 128), F32),
            V((NB, 1, 128), F32),
            V((PLANES, 1, 128), F32),
            V((PLANES, 1, 128), F32),
            V((KB, GRP_DEV), F32),
            D((10,)),
            D((NCHUNK,)),
            D((3,)),
            D((4, 3)),
            D((4, 3)),
            D((2, 2)),
            D((2,)),
            pltpu.SemaphoreType.REGULAR,
        ],
        compiler_params=pltpu.CompilerParams(
            collective_id=0, has_side_effects=True, vmem_limit_bytes=48 << 20
        ),
    )(
        source_cell,
        electric_start,
        magnetic_start,
        current_start,
        cotangent,
        level_set,
        material,
        basis.reshape(NB * KB, TILE),
        block_owner.reshape(1, NB),
        block_group.reshape(1, NB),
    )


def solution(mesh):
    return jax.shard_map(
        local,
        mesh=mesh,
        in_specs=(
            P(None, "by", "bx", "gz"),
            P(None, "by", "bx", "gz"),
            P(None, "by", "bx", "gz"),
            P(None, "by", "bx", "gz"),
            P("by", "bx", "gz"),
            P("by", "bx", "gz"),
            P(("bx", "by", "gz")),
            P(("bx", "by", "gz"), None, None),
            P(("bx", "by", "gz"), None),
            P(("bx", "by", "gz")),
        ),
        out_specs=(
            P(None, "by", "bx", "gz"),
            P(None, "by", "bx", "gz"),
            P(None, ("bx", "by", "gz")),
        ),
        check_vma=False,
    )
```

```python
import jax
import jax.numpy as jnp
from jax import lax
from jax.experimental import pallas as pl
from jax.experimental.pallas import tpu as pltpu
from jax.sharding import PartitionSpec as P

KB = 64
GRP_DEV = 128
NBX = 4
NBY = 32
PLANES = 128
NB = 256
TILES = 128
TILE = 256
NCHUNK = 8

time_step = 0.5
drude_keep = 0.9
drude_gain = 1.0
metal_permit = 3.0
design_contrast = 5.0
source_level = 3.0
source_wave = (1.0, -0.6, 0.8, -0.4)

F32 = jnp.float32
BF16 = jnp.bfloat16
MESH = pl.DeviceIdType.MESH

IDX = {("x", 0): 0, ("z", 0): 1, ("x", 1): 2, ("z", 1): 3, ("y", 0): 4, ("y", 1): 5}
COMP = {"x": 0, "y": 1, "z": 2}


def iota(shape, dim):
    return lax.broadcasted_iota(jnp.int32, shape, dim)


def split(v):
    hi = v.astype(BF16)
    lo = (v - hi.astype(F32)).astype(BF16)
    return hi, lo


def kernel(
    source_ref,
    e0_hbm,
    h0_hbm,
    j0_hbm,
    cot_hbm,
    level_hbm,
    material_hbm,
    basis_hbm,
    owner_hbm,
    group_hbm,
    e_out,
    a_out,
    coef_out,
    p1,
    p2,
    m1,
    m2,
    h0,
    j0,
    cot,
    level,
    material,
    ratio,
    silver,
    factor,
    sources,
    adj1,
    part1,
    grad,
    efin,
    afin,
    basis,
    owner,
    group,
    xsend,
    xrecv,
    zsend,
    zrecv,
    place,
    partial,
    vsend,
    vrecv,
    isend,
    irecv,
    coef,
    in_sem,
    basis_sem,
    out_sem,
    send_sem,
    recv_sem,
    a2a_sem,
    own_sem,
    ready_sem,
):
    bx, by, gz = lax.axis_index("bx"), lax.axis_index("by"), lax.axis_index("gz")
    me = bx * NBY + by
    yy, zz = by // 8, by % 8
    xy = bx * 4 + yy

    loads = [
        (material_hbm, material),
        (level_hbm, level),
        (cot_hbm, cot),
        (e0_hbm.at[0], p1.at[0, pl.ds(0, 16)]),
        (e0_hbm.at[2], p1.at[1, pl.ds(0, 16)]),
        (e0_hbm.at[1], p1.at[4, pl.ds(0, 16)]),
        (h0_hbm, h0),
        (j0_hbm, j0),
        (owner_hbm, owner),
        (group_hbm, group),
    ]
    loads = [pltpu.make_async_copy(s, d, in_sem.at[i]) for i, (s, d) in enumerate(loads)]
    for c in loads:
        c.start()

    zrow = jnp.zeros((4, 16, 128), F32)
    for ref, at in ((p1, 16), (p2, 16), (m1, 0), (m2, 0)):
        ref[0:4, at] = zrow
    for r in range(4):
        xrecv[r] = zrow
        zrecv[r] = jnp.zeros((16, 128), F32)

    barrier = pltpu.get_barrier_semaphore()

    def hail(**where):
        pl.semaphore_signal(barrier, inc=1, device_id=where, device_id_type=MESH)

    for i in range(1, 8):
        hail(by=yy * 8 + (zz + i) % 8)
    for i in range(1, 16):
        q = (xy + i) % 16
        hail(bx=q // 4, by=(q % 4) * 8 + zz)
    hail(gz=1 - gz)
    up_far = jnp.logical_and(zz == 7, by < NBY - 1)
    down_far = jnp.logical_and(zz == 0, by > 0)

    @pl.when(up_far)
    def _():
        hail(by=by + 1)

    @pl.when(down_far)
    def _():
        hail(by=by - 1)

    for c in loads[:6]:
        c.wait()
    bases = [
        pltpu.make_async_copy(
            basis_hbm.at[pl.ds(i * (NB * KB // NCHUNK), NB * KB // NCHUNK)],
            basis.at[pl.ds(i * (NB * KB // NCHUNK), NB * KB // NCHUNK)],
            basis_sem.at[i],
        )
        for i in range(NCHUNK)
    ]
    for c in bases:
        c.start()

    row = iota((16, 128), 0)
    lane = iota((16, 128), 1)

    def pack_z(acc, y, vals, from_lane):
        for c, v in enumerate(vals):
            at = 4 * y + c
            acc = jnp.where(lane == at, pltpu.roll(v, (at + 128 - from_lane) % 128, 1), acc)
        return acc

    def first(y, acc):
        mat = material[y]
        lev = level[y]
        smooth = jax.nn.sigmoid(lev)
        design = (mat == 1).astype(F32)
        sil = (mat == 2).astype(F32)
        permit = jnp.where(mat == 2, metal_permit, jnp.where(mat == 1, 1.0 + design_contrast * smooth, 1.0))
        rat = time_step / permit
        ratio[y] = rat
        silver[y] = sil
        factor[y] = -(design * design_contrast * (smooth * (1.0 - smooth))) / permit
        sx, sy, sz = (rat * cot[c, y] for c in range(3))
        p1[2, y] = sx
        p1[3, y] = sz
        p1[5, y] = sy
        ex, ey, ez = p1[0, y], p1[4, y], p1[1, y]
        for c, v in enumerate((ey, ez, sy, sz)):
            xsend[0, c, pl.ds(y, 1), :] = v[0:1]
        return pack_z(acc, y, (ex, ey, sx, sy), 0)

    zsend[0] = lax.fori_loop(0, 16, first, jnp.zeros((16, 128), F32))

    pl.semaphore_wait(barrier, 23 + up_far.astype(jnp.int32) + down_far.astype(jnp.int32))
    for i in range(1, 16):
        q = (xy + i) % 16
        pl.semaphore_signal(
            ready_sem, inc=1, device_id={"bx": q // 4, "by": (q % 4) * 8 + zz}, device_id_type=MESH
        )

    def moves(r, field):
        plus = r % 2 == 0
        step = -1 if plus else 1
        edge, halo = (0, 16) if plus else (16, 0)

        def move(src, dst, i, **where):
            return pltpu.make_async_remote_copy(
                src_ref=src,
                dst_ref=dst,
                send_sem=send_sem.at[r, i],
                recv_sem=recv_sem.at[r, i],
                device_id=where,
                device_id_type=MESH,
            )

        y_out = by > 0 if plus else by < NBY - 1
        y_in = by < NBY - 1 if plus else by > 0
        x_out = bx > 0 if plus else bx < NBX - 1
        x_in = bx < NBX - 1 if plus else bx > 0
        z_out = gz == 1 if plus else gz == 0
        z_in = gz == 0 if plus else gz == 1
        return (
            (y_out, y_in, move(field.at[pl.ds(0, 4), edge], field.at[pl.ds(0, 4), halo], 0, by=by + step)),
            (x_out, x_in, move(xsend.at[r], xrecv.at[r], 1, bx=bx + step)),
            (z_out, z_in, move(zsend.at[r], zrecv.at[r], 2, gz=1 - gz)),
        )

    def send(r, field):
        for out, _, c in moves(r, field):
            pl.when(out)(c.start)

    def receive(r, field):
        for out, into, c in moves(r, field):
            pl.when(into)(c.wait_recv)
            pl.when(out)(c.wait_send)

    send(0, p1)

    for c in loads[6:]:
        c.wait()

    def count(y, _):
        flat = y * 2048 + row * 128 + lane
        total = jnp.zeros((16, 128), F32)
        for i in range(8):
            total = total + (flat == source_ref[i]).astype(F32)
        sources[y] = total
        return 0

    lax.fori_loop(0, 16, count, 0)

    owner_row = owner[...].astype(F32)
    group_row = group[...].astype(F32)
    ri, ci = iota((NB, NB), 0), iota((NB, NB), 1)
    owner_wide = jnp.broadcast_to(owner_row, (NB, NB))
    owner_col = jnp.sum(jnp.where(ri == ci, owner_wide, 0.0), axis=1, keepdims=True)
    group_col = jnp.sum(jnp.where(ri == ci, jnp.broadcast_to(group_row, (NB, NB)), 0.0), axis=1, keepdims=True)
    same = jnp.logical_and(owner_wide == owner_col, ci < ri)
    rank_col = jnp.sum(same.astype(F32), axis=1, keepdims=True)
    target_col = owner_col * 4.0 + rank_col
    block, tile = iota((NB, TILES), 0), iota((NB, TILES), 1)
    id_sum = jnp.zeros((PLANES, 128), F32)
    dest, id_lane = iota((PLANES, TILES), 0), iota((PLANES, TILES), 1)
    targets, groups = [], []
    for f in range(2):
        pick = block == 2 * tile + f
        targets.append(jnp.sum(jnp.where(pick, target_col, 0.0), axis=0, keepdims=True))
        groups.append(jnp.sum(jnp.where(pick, group_col, 0.0), axis=0, keepdims=True))
    slot_row = (2 * iota((NB, TILES), 0)).astype(F32)
    for h in range(2):
        for f in range(2):
            place[:, pl.ds((2 * h + f) * TILES, TILES)] = (
                (targets[f] == slot_row + float(h)).astype(F32).astype(BF16)
            )
    first_slot = (4 * dest).astype(F32)
    for s in range(4):
        hit = jnp.zeros((PLANES, TILES), F32)
        for f in range(2):
            hit = hit + jnp.where(targets[f] == first_slot + float(s), groups[f], 0.0)
        id_sum = jnp.where(id_lane == s, jnp.sum(hit, axis=1, keepdims=True), id_sum)
    isend[:, 0, :] = id_sum

    def plus_half(r, field, old, out):
        nxt = r + 1

        def body(y, acc):
            zf = zrecv[r]
            vals = {}
            for s in range(2):
                fx, fy, fz = (field[IDX[(c, s)], y] for c in "xyz")
                dyx = field[IDX[("x", s)], y + 1] - fx
                dyz = field[IDX[("z", s)], y + 1] - fz

                def along_x(v, c):
                    return jnp.where(row == 15, xrecv[r, c, pl.ds(y, 1), :], pltpu.roll(v, 15, 0)) - v

                def along_z(v, c):
                    return jnp.where(lane == 127, pltpu.roll(zf, 127 - 4 * y - c, 1), pltpu.roll(v, 127, 1)) - v

                dxy, dxz = along_x(fy, 2 * s), along_x(fz, 2 * s + 1)
                dzx, dzy = along_z(fx, 2 * s), along_z(fy, 2 * s + 1)
                turn = {"x": dyz - dzy, "y": dzx - dxz, "z": dxy - dyx}
                for c in "xyz":
                    new = old(s, c, y, turn[c])
                    out[IDX[(c, s)], y + 1] = new
                    vals[(c, s)] = new
            for i, k in enumerate((("y", 0), ("z", 0), ("y", 1), ("z", 1))):
                xsend[nxt, i, pl.ds(y, 1), :] = vals[k][15:16]
            return pack_z(acc, y, [vals[k] for k in (("x", 0), ("y", 0), ("x", 1), ("y", 1))], 127)

        zsend[nxt] = lax.fori_loop(0, 16, body, jnp.zeros((16, 128), F32))

    def minus_turn(r, field, y, s):
        zf = zrecv[r]
        fx, fy, fz = (field[IDX[(c, s)], y + 1] for c in "xyz")
        dyx = fx - field[IDX[("x", s)], y]
        dyz = fz - field[IDX[("z", s)], y]

        def along_x(v, c):
            return v - jnp.where(row == 0, xrecv[r, c, pl.ds(y, 1), :], pltpu.roll(v, 1, 0))

        def along_z(v, c):
            return v - jnp.where(lane == 0, pltpu.roll(zf, 128 - 4 * y - c, 1), pltpu.roll(v, 1, 1))

        dxy, dxz = along_x(fy, 2 * s), along_x(fz, 2 * s + 1)
        dzx, dzy = along_z(fx, 2 * s), along_z(fy, 2 * s + 1)
        return {"x": dyz - dzy, "y": dzx - dxz, "z": dxy - dyx}

    def old_first(s, c, y, turn):
        return turn if s else h0[COMP[c], y] - time_step * turn

    def old_second(s, c, y, turn):
        before = m1[IDX[(c, s)], y + 1]
        return before + turn if s else before - time_step * turn

    receive(0, p1)
    plus_half(0, p1, old_first, m1)
    send(1, m1)

    pl.semaphore_wait(ready_sem, 15)

    def spread(src, dst, width, k):
        def one(i, _):
            p = (me + i) % PLANES
            pltpu.make_async_remote_copy(
                src_ref=src.at[pl.ds(p * width, width)],
                dst_ref=dst.at[pl.ds(me * width, width)],
                send_sem=a2a_sem.at[k, 0],
                recv_sem=a2a_sem.at[k, 1],
                device_id={"bx": p // NBY, "by": p % NBY},
                device_id_type=MESH,
            ).start()
            return 0

        own = pltpu.make_async_copy(
            src.at[pl.ds(me * width, width)], dst.at[pl.ds(me * width, width)], own_sem.at[k]
        )
        own.start()
        lax.fori_loop(1, PLANES, one, 0, unroll=4)

    def gathered(src, dst, width, k):
        many = pl.ds(0, (PLANES - 1) * width)
        pltpu.make_async_copy(src.at[many], src.at[many], a2a_sem.at[k, 0]).wait()
        pltpu.make_async_copy(dst.at[many], dst.at[many], a2a_sem.at[k, 1]).wait()
        pltpu.make_async_copy(
            src.at[pl.ds(me * width, width)], dst.at[pl.ds(me * width, width)], own_sem.at[k]
        ).wait()

    spread(isend, irecv, 1, 0)

    receive(1, m1)

    def electric_first(y, acc):
        rat, sil = ratio[y], silver[y]
        turn, back = minus_turn(1, m1, y, 0), minus_turn(1, m1, y, 1)
        total = jnp.zeros((16, 128), F32)
        fwd, adj = {}, {}
        for c in "xyz":
            e = p1[IDX[(c, 0)], y]
            cur = sil * (drude_keep * j0[COMP[c], y] + drude_gain * e)
            drive = turn[c] - cur
            j0[COMP[c], y] = cur
            new = e + rat * drive
            if c == "z":
                new = new + source_level * source_wave[0] * sources[y]
            fwd[c] = new
            p2[IDX[(c, 0)], y] = new
            scaled = p1[IDX[(c, 1)], y]
            a = cot[COMP[c], y] - drude_gain * (sil * scaled) - time_step * back[c]
            adj1[COMP[c], y] = a
            s0 = rat * a
            adj[c] = s0
            p2[IDX[(c, 1)], y] = s0
            total = total + s0 * drive
        part1[y] = total
        for i, v in enumerate((fwd["y"], fwd["z"], adj["y"], adj["z"])):
            xsend[2, i, pl.ds(y, 1), :] = v[0:1]
        return pack_z(acc, y, (fwd["x"], fwd["y"], adj["x"], adj["y"]), 0)

    zsend[2] = lax.fori_loop(0, 16, electric_first, jnp.zeros((16, 128), F32))
    send(2, p2)
    receive(2, p2)
    plus_half(2, p2, old_second, m2)
    send(3, m2)
    receive(3, m2)

    def electric_second(y, _):
        rat, sil = ratio[y], silver[y]
        turn, back = minus_turn(3, m2, y, 0), minus_turn(3, m2, y, 1)
        total = part1[y]
        for c in "xyz":
            e = p2[IDX[(c, 0)], y]
            cur = sil * (drude_keep * j0[COMP[c], y] + drude_gain * e)
            drive = turn[c] - cur
            new = e + rat * drive
            if c == "z":
                new = new + source_level * source_wave[1] * sources[y]
            efin[COMP[c], y] = new
            scaled = p1[IDX[(c, 1)], y]
            s0 = p2[IDX[(c, 1)], y]
            adj_drive = -drude_keep * (sil * scaled) - s0
            afin[COMP[c], y] = adj1[COMP[c], y] + drude_gain * (sil * adj_drive) - time_step * back[c]
            total = total + scaled * drive
        grad[pl.ds(pl.multiple_of(y * 16, 16), 16), :] = factor[y] * total
        return 0

    lax.fori_loop(0, 16, electric_second, 0)
    outs = [
        pltpu.make_async_copy(efin, e_out, out_sem.at[0]),
        pltpu.make_async_copy(afin, a_out, out_sem.at[1]),
    ]
    for c in outs:
        c.start()
    for c in bases:
        c.wait()

    low128 = iota((16, 128), 1) < 64
    r256, l256 = iota((16, 256), 0), iota((16, 256), 1)

    def tiles(i, _):
        start = pl.multiple_of(i * 16, 16)
        even = grad[pl.ds(2 * start, 16, stride=2), :]
        odd = grad[pl.ds(2 * start + 1, 16, stride=2), :]
        lhs = jnp.concatenate([even.astype(BF16), odd.astype(BF16)], axis=1)
        acc = jnp.zeros((16, 256), F32)
        for j in range(8):
            w = basis[pl.ds(pl.multiple_of(i * 2048 + j * 256, 256), 256), :]
            got = lax.dot_general(lhs, w, (((1,), (1,)), ((), ())), preferred_element_type=F32)
            acc = jnp.where(r256 == 2 * j + l256 // 128, got, acc)
        partial[pl.ds(start, 16), :] = jnp.where(row % 2 == 0, acc[:, :128], acc[:, 128:])
        return 0

    lax.fori_loop(0, 8, tiles, 0)

    part = partial[...]
    turned = pltpu.roll(part, 64, 1)
    low = iota((TILES, 128), 1) < 64
    stack = jnp.concatenate(
        [
            jnp.where(low, part, 0.0),
            jnp.where(low, turned, 0.0),
            jnp.where(low, 0.0, turned),
            jnp.where(low, 0.0, part),
        ],
        axis=0,
    )
    hi, lo = split(stack)
    slots = lax.dot_general(place[...], hi, (((1,), (0,)), ((), ())), preferred_element_type=F32)
    slots = slots + lax.dot_general(place[...], lo, (((1,), (0,)), ((), ())), preferred_element_type=F32)
    vsend[:, 0, :] = slots
    spread(vsend, vrecv, 2, 1)

    gathered(isend, irecv, 1, 0)
    ids = irecv[:, 0, :]
    group_lane = iota((PLANES, GRP_DEV), 1).astype(F32)
    hits = jnp.concatenate(
        [
            jnp.concatenate(
                [(ids[:, 2 * p + h : 2 * p + h + 1] == group_lane).astype(F32).astype(BF16) for h in range(2)], axis=1
            )
            for p in range(2)
        ],
        axis=0,
    )
    gathered(vsend, vrecv, 2, 1)
    vals = jnp.concatenate([vrecv[pl.ds(p, PLANES, stride=2), 0, :] for p in range(2)], axis=0)
    hi, lo = split(vals)
    both = lax.dot_general(hi, hits, (((0,), (0,)), ((), ())), preferred_element_type=F32)
    both = both + lax.dot_general(lo, hits, (((0,), (0,)), ((), ())), preferred_element_type=F32)
    coef[...] = both[:KB, :GRP_DEV] + both[KB:, GRP_DEV:]
    last = pltpu.make_async_copy(coef, coef_out, out_sem.at[2])
    last.start()
    for c in outs:
        c.wait()
    last.wait()


def local(
    electric_start,
    magnetic_start,
    current_start,
    cotangent,
    level_set,
    material,
    source_cell,
    basis,
    block_owner,
    block_group,
):
    field = (3, 16, 16, 128)
    brick = (16, 16, 128)
    anywhere = pl.BlockSpec(memory_space=pltpu.HBM)
    V, D = pltpu.VMEM, pltpu.SemaphoreType.DMA
    return pl.pallas_call(
        kernel,
        name="adjoint_step",
        out_shape=(
            jax.ShapeDtypeStruct(field, F32),
            jax.ShapeDtypeStruct(field, F32),
            jax.ShapeDtypeStruct((KB, GRP_DEV), F32),
        ),
        in_specs=[pl.BlockSpec(memory_space=pltpu.SMEM)] + [anywhere] * 9,
        out_specs=(anywhere,) * 3,
        scratch_shapes=[
            V((6, 17, 16, 128), F32),
            V((6, 17, 16, 128), F32),
            V((6, 17, 16, 128), F32),
            V((6, 17, 16, 128), F32),
            V(field, F32),
            V(field, F32),
            V(field, F32),
            V(brick, F32),
            V(brick, jnp.int32),
            V(brick, F32),
            V(brick, F32),
            V(brick, F32),
            V(brick, F32),
            V(field, F32),
            V(brick, F32),
            V((256, 128), F32),
            V(field, F32),
            V(field, F32),
            V((NB * KB, TILE), BF16),
            V((1, NB), jnp.int32),
            V((1, NB), jnp.int32),
            V((4, 4, 16, 128), F32),
            V((4, 4, 16, 128), F32),
            V((4, 16, 128), F32),
            V((4, 16, 128), F32),
            V((NB, 4 * TILES), BF16),
            V((TILES, 128), F32),
            V((NB, 1, 128), F32),
            V((NB, 1, 128), F32),
            V((PLANES, 1, 128), F32),
            V((PLANES, 1, 128), F32),
            V((KB, GRP_DEV), F32),
            D((10,)),
            D((NCHUNK,)),
            D((3,)),
            D((4, 3)),
            D((4, 3)),
            D((2, 2)),
            D((2,)),
            pltpu.SemaphoreType.REGULAR,
        ],
        compiler_params=pltpu.CompilerParams(
            collective_id=0, has_side_effects=True, vmem_limit_bytes=56000 << 10
        ),
    )(
        source_cell,
        electric_start,
        magnetic_start,
        current_start,
        cotangent,
        level_set,
        material,
        basis.reshape(NB * KB, TILE),
        block_owner.reshape(1, NB),
        block_group.reshape(1, NB),
    )


def solution(mesh):
    return jax.shard_map(
        local,
        mesh=mesh,
        in_specs=(
            P(None, "by", "bx", "gz"),
            P(None, "by", "bx", "gz"),
            P(None, "by", "bx", "gz"),
            P(None, "by", "bx", "gz"),
            P("by", "bx", "gz"),
            P("by", "bx", "gz"),
            P(("bx", "by", "gz")),
            P(("bx", "by", "gz"), None, None),
            P(("bx", "by", "gz"), None),
            P(("bx", "by", "gz")),
        ),
        out_specs=(
            P(None, "by", "bx", "gz"),
            P(None, "by", "bx", "gz"),
            P(None, ("bx", "by", "gz")),
        ),
        check_vma=False,
    )
```

```python
import jax
import jax.numpy as jnp
from jax import lax
from jax.experimental import pallas as pl
from jax.experimental.pallas import tpu as pltpu
from jax.sharding import PartitionSpec as P

KB = 64
GRP_DEV = 128
NBX = 4
NBY = 32
PLANES = 128
NB = 256
TILES = 128
TILE = 256
NCHUNK = 8

time_step = 0.5
drude_keep = 0.9
drude_gain = 1.0
metal_permit = 3.0
design_contrast = 5.0
source_level = 3.0
source_wave = (1.0, -0.6, 0.8, -0.4)

F32 = jnp.float32
BF16 = jnp.bfloat16
MESH = pl.DeviceIdType.MESH

IDX = {("x", 0): 0, ("z", 0): 1, ("x", 1): 2, ("z", 1): 3, ("y", 0): 4, ("y", 1): 5}
COMP = {"x": 0, "y": 1, "z": 2}


def iota(shape, dim):
    return lax.broadcasted_iota(jnp.int32, shape, dim)


def split(v):
    hi = v.astype(BF16)
    lo = (v - hi.astype(F32)).astype(BF16)
    return hi, lo


def kernel(
    source_ref,
    e0_hbm,
    h0_hbm,
    j0_hbm,
    cot_hbm,
    level_hbm,
    material_hbm,
    basis_hbm,
    owner_hbm,
    group_hbm,
    e_out,
    a_out,
    coef_out,
    p1,
    p2,
    m1,
    m2,
    h0,
    j0,
    cot,
    level,
    material,
    ratio,
    silver,
    factor,
    sources,
    adj1,
    part1,
    grad,
    efin,
    afin,
    basis,
    owner,
    group,
    xsend,
    xrecv,
    zsend,
    zrecv,
    place,
    partial,
    vsend,
    vrecv,
    coef,
    in_sem,
    basis_sem,
    out_sem,
    send_sem,
    recv_sem,
    a2a_sem,
    own_sem,
    ready_sem,
):
    bx, by, gz = lax.axis_index("bx"), lax.axis_index("by"), lax.axis_index("gz")
    me = bx * NBY + by
    yy, zz = by // 8, by % 8
    xy = bx * 4 + yy

    loads = [
        (material_hbm, material),
        (level_hbm, level),
        (cot_hbm, cot),
        (e0_hbm.at[0], p1.at[0, pl.ds(0, 16)]),
        (e0_hbm.at[2], p1.at[1, pl.ds(0, 16)]),
        (e0_hbm.at[1], p1.at[4, pl.ds(0, 16)]),
        (h0_hbm, h0),
        (j0_hbm, j0),
        (owner_hbm, owner),
        (group_hbm, group),
    ]
    loads = [pltpu.make_async_copy(s, d, in_sem.at[i]) for i, (s, d) in enumerate(loads)]
    for c in loads:
        c.start()

    zrow = jnp.zeros((4, 16, 128), F32)
    for ref, at in ((p1, 16), (p2, 16), (m1, 0), (m2, 0)):
        ref[0:4, at] = zrow
    for r in range(4):
        xrecv[r] = zrow
        zrecv[r] = jnp.zeros((16, 128), F32)

    barrier = pltpu.get_barrier_semaphore()

    def hail(**where):
        pl.semaphore_signal(barrier, inc=1, device_id=where, device_id_type=MESH)

    for i in range(1, 8):
        hail(by=yy * 8 + (zz + i) % 8)
    for i in range(1, 16):
        q = (xy + i) % 16
        hail(bx=q // 4, by=(q % 4) * 8 + zz)
    hail(gz=1 - gz)
    up_far = jnp.logical_and(zz == 7, by < NBY - 1)
    down_far = jnp.logical_and(zz == 0, by > 0)

    @pl.when(up_far)
    def _():
        hail(by=by + 1)

    @pl.when(down_far)
    def _():
        hail(by=by - 1)

    for c in loads[:6]:
        c.wait()
    bases = [
        pltpu.make_async_copy(
            basis_hbm.at[pl.ds(i * (NB * KB // NCHUNK), NB * KB // NCHUNK)],
            basis.at[pl.ds(i * (NB * KB // NCHUNK), NB * KB // NCHUNK)],
            basis_sem.at[i],
        )
        for i in range(NCHUNK)
    ]
    for c in bases:
        c.start()

    row = iota((16, 128), 0)
    lane = iota((16, 128), 1)

    def pack_z(acc, y, vals, from_lane):
        for c, v in enumerate(vals):
            at = 4 * y + c
            acc = jnp.where(lane == at, pltpu.roll(v, (at + 128 - from_lane) % 128, 1), acc)
        return acc

    def first(y, acc):
        mat = material[y]
        lev = level[y]
        smooth = jax.nn.sigmoid(lev)
        design = (mat == 1).astype(F32)
        sil = (mat == 2).astype(F32)
        permit = jnp.where(mat == 2, metal_permit, jnp.where(mat == 1, 1.0 + design_contrast * smooth, 1.0))
        rat = time_step / permit
        ratio[y] = rat
        silver[y] = sil
        factor[y] = -(design * design_contrast * (smooth * (1.0 - smooth))) / permit
        sx, sy, sz = (rat * cot[c, y] for c in range(3))
        p1[2, y] = sx
        p1[3, y] = sz
        p1[5, y] = sy
        ex, ey, ez = p1[0, y], p1[4, y], p1[1, y]
        for c, v in enumerate((ey, ez, sy, sz)):
            xsend[0, c, pl.ds(y, 1), :] = v[0:1]
        return pack_z(acc, y, (ex, ey, sx, sy), 0)

    zsend[0] = lax.fori_loop(0, 16, first, jnp.zeros((16, 128), F32))

    pl.semaphore_wait(barrier, 23 + up_far.astype(jnp.int32) + down_far.astype(jnp.int32))
    for i in range(1, 16):
        q = (xy + i) % 16
        pl.semaphore_signal(
            ready_sem, inc=1, device_id={"bx": q // 4, "by": (q % 4) * 8 + zz}, device_id_type=MESH
        )

    def moves(r, field):
        plus = r % 2 == 0
        step = -1 if plus else 1
        edge, halo = (0, 16) if plus else (16, 0)

        def move(src, dst, i, **where):
            return pltpu.make_async_remote_copy(
                src_ref=src,
                dst_ref=dst,
                send_sem=send_sem.at[r, i],
                recv_sem=recv_sem.at[r, i],
                device_id=where,
                device_id_type=MESH,
            )

        y_out = by > 0 if plus else by < NBY - 1
        y_in = by < NBY - 1 if plus else by > 0
        x_out = bx > 0 if plus else bx < NBX - 1
        x_in = bx < NBX - 1 if plus else bx > 0
        z_out = gz == 1 if plus else gz == 0
        z_in = gz == 0 if plus else gz == 1
        return (
            (y_out, y_in, move(field.at[pl.ds(0, 4), edge], field.at[pl.ds(0, 4), halo], 0, by=by + step)),
            (x_out, x_in, move(xsend.at[r], xrecv.at[r], 1, bx=bx + step)),
            (z_out, z_in, move(zsend.at[r], zrecv.at[r], 2, gz=1 - gz)),
        )

    def send(r, field):
        for out, _, c in moves(r, field):
            pl.when(out)(c.start)

    def receive(r, field, first, last):
        for _, into, c in moves(r, field)[first:last]:
            pl.when(into)(c.wait_recv)

    def sent(r, field):
        for out, _, c in moves(r, field):
            pl.when(out)(c.wait_send)

    send(0, p1)

    for c in loads[6:]:
        c.wait()

    def count(y, _):
        flat = y * 2048 + row * 128 + lane
        total = jnp.zeros((16, 128), F32)
        for i in range(8):
            total = total + (flat == source_ref[i]).astype(F32)
        sources[y] = total
        return 0

    lax.fori_loop(0, 16, count, 0)

    owner_row = owner[...].astype(F32)
    group_row = group[...].astype(F32)
    ri, ci = iota((NB, NB), 0), iota((NB, NB), 1)
    owner_wide = jnp.broadcast_to(owner_row, (NB, NB))
    owner_col = jnp.sum(jnp.where(ri == ci, owner_wide, 0.0), axis=1, keepdims=True)
    group_col = jnp.sum(jnp.where(ri == ci, jnp.broadcast_to(group_row, (NB, NB)), 0.0), axis=1, keepdims=True)
    same = jnp.logical_and(owner_wide == owner_col, ci < ri)
    rank_col = jnp.sum(same.astype(F32), axis=1, keepdims=True)
    target_col = owner_col * 4.0 + rank_col
    block, tile = iota((NB, TILES), 0), iota((NB, TILES), 1)
    id_sum = jnp.zeros((PLANES, 128), F32)
    dest, id_lane = iota((PLANES, TILES), 0), iota((PLANES, TILES), 1)
    targets, groups = [], []
    for f in range(2):
        pick = block == 2 * tile + f
        targets.append(jnp.sum(jnp.where(pick, target_col, 0.0), axis=0, keepdims=True))
        groups.append(jnp.sum(jnp.where(pick, group_col, 0.0), axis=0, keepdims=True))
    slot_row = (4 * (block % PLANES) + 2 * (block // PLANES)).astype(F32)
    for h in range(2):
        for f in range(2):
            place[:, pl.ds((2 * h + f) * TILES, TILES)] = (
                (targets[f] == slot_row + float(h)).astype(F32).astype(BF16)
            )
    first_slot = (4 * dest).astype(F32)
    for s in range(4):
        hit = jnp.zeros((PLANES, TILES), F32)
        for f in range(2):
            hit = hit + jnp.where(targets[f] == first_slot + float(s), groups[f], 0.0)
        id_sum = jnp.where(id_lane == s, jnp.sum(hit, axis=1, keepdims=True), id_sum)
    vsend[pl.ds(2, PLANES, stride=3), 0, :] = id_sum

    def plus_half(r, field, old, out):
        nxt = r + 1

        def body(y, acc):
            zf = zrecv[r]
            vals = {}
            for s in range(2):
                fx, fy, fz = (field[IDX[(c, s)], y] for c in "xyz")
                dyx = field[IDX[("x", s)], y + 1] - fx
                dyz = field[IDX[("z", s)], y + 1] - fz

                def along_x(v, c):
                    return jnp.where(row == 15, xrecv[r, c, pl.ds(y, 1), :], pltpu.roll(v, 15, 0)) - v

                def along_z(v, c):
                    return jnp.where(lane == 127, pltpu.roll(zf, 127 - 4 * y - c, 1), pltpu.roll(v, 127, 1)) - v

                dxy, dxz = along_x(fy, 2 * s), along_x(fz, 2 * s + 1)
                dzx, dzy = along_z(fx, 2 * s), along_z(fy, 2 * s + 1)
                turn = {"x": dyz - dzy, "y": dzx - dxz, "z": dxy - dyx}
                for c in "xyz":
                    new = old(s, c, y, turn[c])
                    out[IDX[(c, s)], y + 1] = new
                    vals[(c, s)] = new
            for i, k in enumerate((("y", 0), ("z", 0), ("y", 1), ("z", 1))):
                xsend[nxt, i, pl.ds(y, 1), :] = vals[k][15:16]
            return pack_z(acc, y, [vals[k] for k in (("x", 0), ("y", 0), ("x", 1), ("y", 1))], 127)

        receive(r, field, 1, 3)
        acc = lax.fori_loop(0, 15, body, jnp.zeros((16, 128), F32))
        receive(r, field, 0, 1)
        zsend[nxt] = body(15, acc)

    def minus_turn(r, field, y, s):
        zf = zrecv[r]
        fx, fy, fz = (field[IDX[(c, s)], y + 1] for c in "xyz")
        dyx = fx - field[IDX[("x", s)], y]
        dyz = fz - field[IDX[("z", s)], y]

        def along_x(v, c):
            return v - jnp.where(row == 0, xrecv[r, c, pl.ds(y, 1), :], pltpu.roll(v, 1, 0))

        def along_z(v, c):
            return v - jnp.where(lane == 0, pltpu.roll(zf, 128 - 4 * y - c, 1), pltpu.roll(v, 1, 1))

        dxy, dxz = along_x(fy, 2 * s), along_x(fz, 2 * s + 1)
        dzx, dzy = along_z(fx, 2 * s), along_z(fy, 2 * s + 1)
        return {"x": dyz - dzy, "y": dzx - dxz, "z": dxy - dyx}

    def old_first(s, c, y, turn):
        return turn if s else h0[COMP[c], y] - time_step * turn

    def old_second(s, c, y, turn):
        before = m1[IDX[(c, s)], y + 1]
        return before + turn if s else before - time_step * turn

    plus_half(0, p1, old_first, m1)
    send(1, m1)

    def chunk(p):
        return pl.ds(p * 3, 3)

    def mine():
        return pltpu.make_async_copy(vsend.at[chunk(me)], vrecv.at[chunk(me)], own_sem)

    def spread():
        def one(i, _):
            p = (me + i) % PLANES
            pltpu.make_async_remote_copy(
                src_ref=vsend.at[chunk(p)],
                dst_ref=vrecv.at[chunk(me)],
                send_sem=a2a_sem.at[0],
                recv_sem=a2a_sem.at[1],
                device_id={"bx": p // NBY, "by": p % NBY},
                device_id_type=MESH,
            ).start()
            return 0

        mine().start()
        lax.fori_loop(1, PLANES, one, 0, unroll=4)

    def gathered():
        many = pl.ds(0, (PLANES - 1) * 3)
        pltpu.make_async_copy(vrecv.at[many], vrecv.at[many], a2a_sem.at[1]).wait()
        mine().wait()

    def all_sent():
        many = pl.ds(0, (PLANES - 1) * 3)
        pltpu.make_async_copy(vsend.at[many], vsend.at[many], a2a_sem.at[0]).wait()

    def electric_first(y, acc):
        rat, sil = ratio[y], silver[y]
        turn, back = minus_turn(1, m1, y, 0), minus_turn(1, m1, y, 1)
        total = jnp.zeros((16, 128), F32)
        fwd, adj = {}, {}
        for c in "xyz":
            e = p1[IDX[(c, 0)], y]
            cur = sil * (drude_keep * j0[COMP[c], y] + drude_gain * e)
            drive = turn[c] - cur
            j0[COMP[c], y] = cur
            new = e + rat * drive
            if c == "z":
                new = new + source_level * source_wave[0] * sources[y]
            fwd[c] = new
            p2[IDX[(c, 0)], y] = new
            scaled = p1[IDX[(c, 1)], y]
            a = cot[COMP[c], y] - drude_gain * (sil * scaled) - time_step * back[c]
            adj1[COMP[c], y] = a
            s0 = rat * a
            adj[c] = s0
            p2[IDX[(c, 1)], y] = s0
            total = total + s0 * drive
        part1[y] = total
        for i, v in enumerate((fwd["y"], fwd["z"], adj["y"], adj["z"])):
            xsend[2, i, pl.ds(y, 1), :] = v[0:1]
        return pack_z(acc, y, (fwd["x"], fwd["y"], adj["x"], adj["y"]), 0)

    receive(1, m1, 1, 3)
    pack = lax.fori_loop(1, 16, electric_first, jnp.zeros((16, 128), F32))
    receive(1, m1, 0, 1)
    zsend[2] = electric_first(0, pack)
    send(2, p2)
    plus_half(2, p2, old_second, m2)
    send(3, m2)

    def electric_second(y, _):
        rat, sil = ratio[y], silver[y]
        turn, back = minus_turn(3, m2, y, 0), minus_turn(3, m2, y, 1)
        total = part1[y]
        for c in "xyz":
            e = p2[IDX[(c, 0)], y]
            cur = sil * (drude_keep * j0[COMP[c], y] + drude_gain * e)
            drive = turn[c] - cur
            new = e + rat * drive
            if c == "z":
                new = new + source_level * source_wave[1] * sources[y]
            efin[COMP[c], y] = new
            scaled = p1[IDX[(c, 1)], y]
            s0 = p2[IDX[(c, 1)], y]
            adj_drive = -drude_keep * (sil * scaled) - s0
            afin[COMP[c], y] = adj1[COMP[c], y] + drude_gain * (sil * adj_drive) - time_step * back[c]
            total = total + scaled * drive
        grad[pl.ds(pl.multiple_of(y * 16, 16), 16), :] = factor[y] * total
        return 0

    receive(3, m2, 1, 3)
    lax.fori_loop(1, 16, electric_second, 0)
    receive(3, m2, 0, 1)
    electric_second(0, 0)
    outs = [
        pltpu.make_async_copy(efin, e_out, out_sem.at[0]),
        pltpu.make_async_copy(afin, a_out, out_sem.at[1]),
    ]
    for c in outs:
        c.start()
    for c in bases:
        c.wait()

    low128 = iota((16, 128), 1) < 64
    r256, l256 = iota((16, 256), 0), iota((16, 256), 1)

    def tiles(i, _):
        start = pl.multiple_of(i * 16, 16)
        even = grad[pl.ds(2 * start, 16, stride=2), :]
        odd = grad[pl.ds(2 * start + 1, 16, stride=2), :]
        lhs = jnp.concatenate([even.astype(BF16), odd.astype(BF16)], axis=1)
        acc = jnp.zeros((16, 256), F32)
        for j in range(8):
            w = basis[pl.ds(pl.multiple_of(i * 2048 + j * 256, 256), 256), :]
            got = lax.dot_general(lhs, w, (((1,), (1,)), ((), ())), preferred_element_type=F32)
            acc = jnp.where(r256 == 2 * j + l256 // 128, got, acc)
        partial[pl.ds(start, 16), :] = jnp.where(row % 2 == 0, acc[:, :128], acc[:, 128:])
        return 0

    lax.fori_loop(0, 8, tiles, 0)

    part = partial[...]
    turned = pltpu.roll(part, 64, 1)
    low = iota((TILES, 128), 1) < 64
    stack = jnp.concatenate(
        [
            jnp.where(low, part, 0.0),
            jnp.where(low, turned, 0.0),
            jnp.where(low, 0.0, turned),
            jnp.where(low, 0.0, part),
        ],
        axis=0,
    )
    hi, lo = split(stack)
    slots = lax.dot_general(place[...], hi, (((1,), (0,)), ((), ())), preferred_element_type=F32)
    slots = slots + lax.dot_general(place[...], lo, (((1,), (0,)), ((), ())), preferred_element_type=F32)
    for p in range(2):
        vsend[pl.ds(p, PLANES, stride=3), 0, :] = slots[p * PLANES : (p + 1) * PLANES]
    pl.semaphore_wait(ready_sem, 15)
    spread()

    gathered()
    ids = vrecv[pl.ds(2, PLANES, stride=3), 0, :]
    group_lane = iota((PLANES, GRP_DEV), 1).astype(F32)
    hits = jnp.concatenate(
        [
            jnp.concatenate(
                [(ids[:, 2 * p + h : 2 * p + h + 1] == group_lane).astype(F32).astype(BF16) for h in range(2)], axis=1
            )
            for p in range(2)
        ],
        axis=0,
    )
    vals = jnp.concatenate([vrecv[pl.ds(p, PLANES, stride=3), 0, :] for p in range(2)], axis=0)
    hi, lo = split(vals)
    both = lax.dot_general(hi, hits, (((0,), (0,)), ((), ())), preferred_element_type=F32)
    both = both + lax.dot_general(lo, hits, (((0,), (0,)), ((), ())), preferred_element_type=F32)
    coef[...] = both[:KB, :GRP_DEV] + both[KB:, GRP_DEV:]
    last = pltpu.make_async_copy(coef, coef_out, out_sem.at[2])
    last.start()
    for c in outs:
        c.wait()
    for r, field in enumerate((p1, m1, p2, m2)):
        sent(r, field)
    all_sent()
    last.wait()


def local(
    electric_start,
    magnetic_start,
    current_start,
    cotangent,
    level_set,
    material,
    source_cell,
    basis,
    block_owner,
    block_group,
):
    field = (3, 16, 16, 128)
    brick = (16, 16, 128)
    anywhere = pl.BlockSpec(memory_space=pltpu.HBM)
    V, D = pltpu.VMEM, pltpu.SemaphoreType.DMA
    return pl.pallas_call(
        kernel,
        name="adjoint_step",
        out_shape=(
            jax.ShapeDtypeStruct(field, F32),
            jax.ShapeDtypeStruct(field, F32),
            jax.ShapeDtypeStruct((KB, GRP_DEV), F32),
        ),
        in_specs=[pl.BlockSpec(memory_space=pltpu.SMEM)] + [anywhere] * 9,
        out_specs=(anywhere,) * 3,
        scratch_shapes=[
            V((6, 17, 16, 128), F32),
            V((6, 17, 16, 128), F32),
            V((6, 17, 16, 128), F32),
            V((6, 17, 16, 128), F32),
            V(field, F32),
            V(field, F32),
            V(field, F32),
            V(brick, F32),
            V(brick, jnp.int32),
            V(brick, F32),
            V(brick, F32),
            V(brick, F32),
            V(brick, F32),
            V(field, F32),
            V(brick, F32),
            V((256, 128), F32),
            V(field, F32),
            V(field, F32),
            V((NB * KB, TILE), BF16),
            V((1, NB), jnp.int32),
            V((1, NB), jnp.int32),
            V((4, 4, 16, 128), F32),
            V((4, 4, 16, 128), F32),
            V((4, 16, 128), F32),
            V((4, 16, 128), F32),
            V((NB, 4 * TILES), BF16),
            V((TILES, 128), F32),
            V((3 * PLANES, 1, 128), F32),
            V((3 * PLANES, 1, 128), F32),
            V((KB, GRP_DEV), F32),
            D((10,)),
            D((NCHUNK,)),
            D((3,)),
            D((4, 3)),
            D((4, 3)),
            D((2,)),
            D,
            pltpu.SemaphoreType.REGULAR,
        ],
        compiler_params=pltpu.CompilerParams(
            collective_id=0, has_side_effects=True, vmem_limit_bytes=56000 << 10
        ),
    )(
        source_cell,
        electric_start,
        magnetic_start,
        current_start,
        cotangent,
        level_set,
        material,
        basis.reshape(NB * KB, TILE),
        block_owner.reshape(1, NB),
        block_group.reshape(1, NB),
    )


def solution(mesh):
    return jax.shard_map(
        local,
        mesh=mesh,
        in_specs=(
            P(None, "by", "bx", "gz"),
            P(None, "by", "bx", "gz"),
            P(None, "by", "bx", "gz"),
            P(None, "by", "bx", "gz"),
            P("by", "bx", "gz"),
            P("by", "bx", "gz"),
            P(("bx", "by", "gz")),
            P(("bx", "by", "gz"), None, None),
            P(("bx", "by", "gz"), None),
            P(("bx", "by", "gz")),
        ),
        out_specs=(
            P(None, "by", "bx", "gz"),
            P(None, "by", "bx", "gz"),
            P(None, ("bx", "by", "gz")),
        ),
        check_vma=False,
    )
```

```python
import jax
import jax.numpy as jnp
from jax import lax
from jax.experimental import pallas as pl
from jax.experimental.pallas import tpu as pltpu
from jax.sharding import PartitionSpec as P

KB = 64
GRP_DEV = 128
NBX = 4
NBY = 32
PLANES = 128
NB = 256
TILES = 128
TILE = 256
NCHUNK = 8

time_step = 0.5
drude_keep = 0.9
drude_gain = 1.0
metal_permit = 3.0
design_contrast = 5.0
source_level = 3.0
source_wave = (1.0, -0.6, 0.8, -0.4)

F32 = jnp.float32
BF16 = jnp.bfloat16
MESH = pl.DeviceIdType.MESH

IDX = {("x", 0): 0, ("z", 0): 1, ("x", 1): 2, ("z", 1): 3, ("y", 0): 4, ("y", 1): 5}
COMP = {"x": 0, "y": 1, "z": 2}


def iota(shape, dim):
    return lax.broadcasted_iota(jnp.int32, shape, dim)


def split(v):
    hi = v.astype(BF16)
    lo = (v - hi.astype(F32)).astype(BF16)
    return hi, lo


def kernel(
    source_ref,
    e0_hbm,
    h0_hbm,
    j0_hbm,
    cot_hbm,
    level_hbm,
    material_hbm,
    basis_hbm,
    owner_hbm,
    group_hbm,
    e_out,
    a_out,
    coef_out,
    p1,
    p2,
    m1,
    m2,
    h0,
    j0,
    cot,
    level,
    material,
    ratio,
    silver,
    factor,
    sources,
    adj1,
    part1,
    grad,
    efin,
    afin,
    basis,
    owner,
    group,
    xsend,
    xrecv,
    zsend,
    zrecv,
    place,
    partial,
    vsend,
    vrecv,
    coef,
    in_sem,
    basis_sem,
    out_sem,
    send_sem,
    recv_sem,
    a2a_sem,
    own_sem,
    ready_sem,
):
    bx, by, gz = lax.axis_index("bx"), lax.axis_index("by"), lax.axis_index("gz")
    me = bx * NBY + by
    yy, zz = by // 8, by % 8
    xy = bx * 4 + yy

    loads = [
        (material_hbm, material),
        (level_hbm, level),
        (cot_hbm, cot),
        (e0_hbm.at[0], p1.at[0, pl.ds(0, 16)]),
        (e0_hbm.at[2], p1.at[1, pl.ds(0, 16)]),
        (e0_hbm.at[1], p1.at[4, pl.ds(0, 16)]),
        (h0_hbm, h0),
        (j0_hbm, j0),
        (owner_hbm, owner),
        (group_hbm, group),
    ]
    loads = [pltpu.make_async_copy(s, d, in_sem.at[i]) for i, (s, d) in enumerate(loads)]
    for c in loads:
        c.start()

    zrow = jnp.zeros((4, 16, 128), F32)
    for ref, at in ((p1, 16), (p2, 16), (m1, 0), (m2, 0)):
        ref[0:4, at] = zrow
    for r in range(4):
        xrecv[r] = zrow
        zrecv[r] = jnp.zeros((16, 128), F32)

    barrier = pltpu.get_barrier_semaphore()

    def hail(**where):
        pl.semaphore_signal(barrier, inc=1, device_id=where, device_id_type=MESH)

    for i in range(1, 8):
        hail(by=yy * 8 + (zz + i) % 8)
    for i in range(1, 16):
        q = (xy + i) % 16
        hail(bx=q // 4, by=(q % 4) * 8 + zz)
    hail(gz=1 - gz)
    up_far = jnp.logical_and(zz == 7, by < NBY - 1)
    down_far = jnp.logical_and(zz == 0, by > 0)

    @pl.when(up_far)
    def _():
        hail(by=by + 1)

    @pl.when(down_far)
    def _():
        hail(by=by - 1)

    for c in loads[:6]:
        c.wait()
    bases = [
        pltpu.make_async_copy(
            basis_hbm.at[pl.ds(i * (NB * KB // NCHUNK), NB * KB // NCHUNK)],
            basis.at[pl.ds(i * (NB * KB // NCHUNK), NB * KB // NCHUNK)],
            basis_sem.at[i],
        )
        for i in range(NCHUNK)
    ]
    for c in bases:
        c.start()

    row = iota((16, 128), 0)
    lane = iota((16, 128), 1)

    def pack_z(acc, y, vals, from_lane):
        for c, v in enumerate(vals):
            at = 4 * y + c
            acc = jnp.where(lane == at, pltpu.roll(v, (at + 128 - from_lane) % 128, 1), acc)
        return acc

    def first(y, acc):
        mat = material[y]
        lev = level[y]
        smooth = jax.nn.sigmoid(lev)
        design = (mat == 1).astype(F32)
        sil = (mat == 2).astype(F32)
        permit = jnp.where(mat == 2, metal_permit, jnp.where(mat == 1, 1.0 + design_contrast * smooth, 1.0))
        rat = time_step / permit
        ratio[y] = rat
        silver[y] = sil
        factor[y] = -(design * design_contrast * (smooth * (1.0 - smooth))) / permit
        sx, sy, sz = (rat * cot[c, y] for c in range(3))
        p1[2, y] = sx
        p1[3, y] = sz
        p1[5, y] = sy
        ex, ey, ez = p1[0, y], p1[4, y], p1[1, y]
        for c, v in enumerate((ey, ez, sy, sz)):
            xsend[0, c, pl.ds(y, 1), :] = v[0:1]
        return pack_z(acc, y, (ex, ey, sx, sy), 0)

    zsend[0] = lax.fori_loop(0, 16, first, jnp.zeros((16, 128), F32), unroll=4)

    pl.semaphore_wait(barrier, 23 + up_far.astype(jnp.int32) + down_far.astype(jnp.int32))
    for i in range(1, 16):
        q = (xy + i) % 16
        pl.semaphore_signal(
            ready_sem, inc=1, device_id={"bx": q // 4, "by": (q % 4) * 8 + zz}, device_id_type=MESH
        )

    def moves(r, field):
        plus = r % 2 == 0
        step = -1 if plus else 1
        edge, halo = (0, 16) if plus else (16, 0)

        def move(src, dst, i, **where):
            return pltpu.make_async_remote_copy(
                src_ref=src,
                dst_ref=dst,
                send_sem=send_sem.at[r, i],
                recv_sem=recv_sem.at[r, i],
                device_id=where,
                device_id_type=MESH,
            )

        y_out = by > 0 if plus else by < NBY - 1
        y_in = by < NBY - 1 if plus else by > 0
        x_out = bx > 0 if plus else bx < NBX - 1
        x_in = bx < NBX - 1 if plus else bx > 0
        z_out = gz == 1 if plus else gz == 0
        z_in = gz == 0 if plus else gz == 1
        return (
            (y_out, y_in, move(field.at[pl.ds(0, 4), edge], field.at[pl.ds(0, 4), halo], 0, by=by + step)),
            (x_out, x_in, move(xsend.at[r], xrecv.at[r], 1, bx=bx + step)),
            (z_out, z_in, move(zsend.at[r], zrecv.at[r], 2, gz=1 - gz)),
        )

    def send(r, field):
        for out, _, c in moves(r, field):
            pl.when(out)(c.start)

    def receive(r, field, first, last):
        for _, into, c in moves(r, field)[first:last]:
            pl.when(into)(c.wait_recv)

    def sent(r, field):
        for out, _, c in moves(r, field):
            pl.when(out)(c.wait_send)

    send(0, p1)

    for c in loads[6:]:
        c.wait()

    def count(y, _):
        flat = y * 2048 + row * 128 + lane
        total = jnp.zeros((16, 128), F32)
        for i in range(8):
            total = total + (flat == source_ref[i]).astype(F32)
        sources[y] = total
        return 0

    lax.fori_loop(0, 16, count, 0, unroll=4)

    owner_row = owner[...].astype(F32)
    group_row = group[...].astype(F32)
    ri, ci = iota((NB, NB), 0), iota((NB, NB), 1)
    owner_wide = jnp.broadcast_to(owner_row, (NB, NB))
    owner_col = jnp.sum(jnp.where(ri == ci, owner_wide, 0.0), axis=1, keepdims=True)
    group_col = jnp.sum(jnp.where(ri == ci, jnp.broadcast_to(group_row, (NB, NB)), 0.0), axis=1, keepdims=True)
    same = jnp.logical_and(owner_wide == owner_col, ci < ri)
    rank_col = jnp.sum(same.astype(F32), axis=1, keepdims=True)
    target_col = owner_col * 4.0 + rank_col
    block, tile = iota((NB, TILES), 0), iota((NB, TILES), 1)
    id_sum = jnp.zeros((PLANES, 128), F32)
    dest, id_lane = iota((PLANES, TILES), 0), iota((PLANES, TILES), 1)
    targets, groups = [], []
    for f in range(2):
        pick = block == 2 * tile + f
        targets.append(jnp.sum(jnp.where(pick, target_col, 0.0), axis=0, keepdims=True))
        groups.append(jnp.sum(jnp.where(pick, group_col, 0.0), axis=0, keepdims=True))
    slot_row = (4 * (block % PLANES) + 2 * (block // PLANES)).astype(F32)
    for h in range(2):
        for f in range(2):
            place[:, pl.ds((2 * h + f) * TILES, TILES)] = (
                (targets[f] == slot_row + float(h)).astype(F32).astype(BF16)
            )
    first_slot = (4 * dest).astype(F32)
    for s in range(4):
        hit = jnp.zeros((PLANES, TILES), F32)
        for f in range(2):
            hit = hit + jnp.where(targets[f] == first_slot + float(s), groups[f], 0.0)
        id_sum = jnp.where(id_lane == s, jnp.sum(hit, axis=1, keepdims=True), id_sum)
    vsend[pl.ds(2, PLANES, stride=3), 0, :] = id_sum

    def plus_half(r, field, old, out):
        nxt = r + 1

        def body(y, acc):
            zf = zrecv[r]
            vals = {}
            for s in range(2):
                fx, fy, fz = (field[IDX[(c, s)], y] for c in "xyz")
                dyx = field[IDX[("x", s)], y + 1] - fx
                dyz = field[IDX[("z", s)], y + 1] - fz

                def along_x(v, c):
                    return jnp.where(row == 15, xrecv[r, c, pl.ds(y, 1), :], pltpu.roll(v, 15, 0)) - v

                def along_z(v, c):
                    return jnp.where(lane == 127, pltpu.roll(zf, 127 - 4 * y - c, 1), pltpu.roll(v, 127, 1)) - v

                dxy, dxz = along_x(fy, 2 * s), along_x(fz, 2 * s + 1)
                dzx, dzy = along_z(fx, 2 * s), along_z(fy, 2 * s + 1)
                turn = {"x": dyz - dzy, "y": dzx - dxz, "z": dxy - dyx}
                for c in "xyz":
                    new = old(s, c, y, turn[c])
                    out[IDX[(c, s)], y + 1] = new
                    vals[(c, s)] = new
            for i, k in enumerate((("y", 0), ("z", 0), ("y", 1), ("z", 1))):
                xsend[nxt, i, pl.ds(y, 1), :] = vals[k][15:16]
            return pack_z(acc, y, [vals[k] for k in (("x", 0), ("y", 0), ("x", 1), ("y", 1))], 127)

        receive(r, field, 1, 3)
        acc = lax.fori_loop(0, 15, body, jnp.zeros((16, 128), F32), unroll=5)
        receive(r, field, 0, 1)
        zsend[nxt] = body(15, acc)

    def minus_turn(r, field, y, s):
        zf = zrecv[r]
        fx, fy, fz = (field[IDX[(c, s)], y + 1] for c in "xyz")
        dyx = fx - field[IDX[("x", s)], y]
        dyz = fz - field[IDX[("z", s)], y]

        def along_x(v, c):
            return v - jnp.where(row == 0, xrecv[r, c, pl.ds(y, 1), :], pltpu.roll(v, 1, 0))

        def along_z(v, c):
            return v - jnp.where(lane == 0, pltpu.roll(zf, 128 - 4 * y - c, 1), pltpu.roll(v, 1, 1))

        dxy, dxz = along_x(fy, 2 * s), along_x(fz, 2 * s + 1)
        dzx, dzy = along_z(fx, 2 * s), along_z(fy, 2 * s + 1)
        return {"x": dyz - dzy, "y": dzx - dxz, "z": dxy - dyx}

    def old_first(s, c, y, turn):
        return turn if s else h0[COMP[c], y] - time_step * turn

    def old_second(s, c, y, turn):
        before = m1[IDX[(c, s)], y + 1]
        return before + turn if s else before - time_step * turn

    plus_half(0, p1, old_first, m1)
    send(1, m1)

    def chunk(p):
        return pl.ds(p * 3, 3)

    def mine():
        return pltpu.make_async_copy(vsend.at[chunk(me)], vrecv.at[chunk(me)], own_sem)

    def spread():
        def one(i, _):
            p = (me + i) % PLANES
            pltpu.make_async_remote_copy(
                src_ref=vsend.at[chunk(p)],
                dst_ref=vrecv.at[chunk(me)],
                send_sem=a2a_sem.at[0],
                recv_sem=a2a_sem.at[1],
                device_id={"bx": p // NBY, "by": p % NBY},
                device_id_type=MESH,
            ).start()
            return 0

        mine().start()
        lax.fori_loop(1, PLANES, one, 0, unroll=4)

    def gathered():
        many = pl.ds(0, (PLANES - 1) * 3)
        pltpu.make_async_copy(vrecv.at[many], vrecv.at[many], a2a_sem.at[1]).wait()
        mine().wait()

    def all_sent():
        many = pl.ds(0, (PLANES - 1) * 3)
        pltpu.make_async_copy(vsend.at[many], vsend.at[many], a2a_sem.at[0]).wait()

    def electric_first(y, acc):
        rat, sil = ratio[y], silver[y]
        turn, back = minus_turn(1, m1, y, 0), minus_turn(1, m1, y, 1)
        total = jnp.zeros((16, 128), F32)
        fwd, adj = {}, {}
        for c in "xyz":
            e = p1[IDX[(c, 0)], y]
            cur = sil * (drude_keep * j0[COMP[c], y] + drude_gain * e)
            drive = turn[c] - cur
            j0[COMP[c], y] = cur
            new = e + rat * drive
            if c == "z":
                new = new + source_level * source_wave[0] * sources[y]
            fwd[c] = new
            p2[IDX[(c, 0)], y] = new
            scaled = p1[IDX[(c, 1)], y]
            a = cot[COMP[c], y] - drude_gain * (sil * scaled) - time_step * back[c]
            adj1[COMP[c], y] = a
            s0 = rat * a
            adj[c] = s0
            p2[IDX[(c, 1)], y] = s0
            total = total + s0 * drive
        part1[y] = total
        for i, v in enumerate((fwd["y"], fwd["z"], adj["y"], adj["z"])):
            xsend[2, i, pl.ds(y, 1), :] = v[0:1]
        return pack_z(acc, y, (fwd["x"], fwd["y"], adj["x"], adj["y"]), 0)

    receive(1, m1, 1, 3)
    pack = lax.fori_loop(1, 16, electric_first, jnp.zeros((16, 128), F32), unroll=5)
    receive(1, m1, 0, 1)
    zsend[2] = electric_first(0, pack)
    send(2, p2)
    plus_half(2, p2, old_second, m2)
    send(3, m2)

    def electric_second(y, _):
        rat, sil = ratio[y], silver[y]
        turn, back = minus_turn(3, m2, y, 0), minus_turn(3, m2, y, 1)
        total = part1[y]
        for c in "xyz":
            e = p2[IDX[(c, 0)], y]
            cur = sil * (drude_keep * j0[COMP[c], y] + drude_gain * e)
            drive = turn[c] - cur
            new = e + rat * drive
            if c == "z":
                new = new + source_level * source_wave[1] * sources[y]
            efin[COMP[c], y] = new
            scaled = p1[IDX[(c, 1)], y]
            s0 = p2[IDX[(c, 1)], y]
            adj_drive = -drude_keep * (sil * scaled) - s0
            afin[COMP[c], y] = adj1[COMP[c], y] + drude_gain * (sil * adj_drive) - time_step * back[c]
            total = total + scaled * drive
        grad[pl.ds(pl.multiple_of(y * 16, 16), 16), :] = factor[y] * total
        return 0

    receive(3, m2, 1, 3)
    lax.fori_loop(1, 16, electric_second, 0, unroll=5)
    receive(3, m2, 0, 1)
    electric_second(0, 0)
    outs = [
        pltpu.make_async_copy(efin, e_out, out_sem.at[0]),
        pltpu.make_async_copy(afin, a_out, out_sem.at[1]),
    ]
    for c in outs:
        c.start()
    for c in bases:
        c.wait()

    low128 = iota((16, 128), 1) < 64
    r256, l256 = iota((16, 256), 0), iota((16, 256), 1)

    def tiles(i, _):
        start = pl.multiple_of(i * 16, 16)
        even = grad[pl.ds(2 * start, 16, stride=2), :]
        odd = grad[pl.ds(2 * start + 1, 16, stride=2), :]
        lhs = jnp.concatenate([even.astype(BF16), odd.astype(BF16)], axis=1)
        acc = jnp.zeros((16, 256), F32)
        for j in range(8):
            w = basis[pl.ds(pl.multiple_of(i * 2048 + j * 256, 256), 256), :]
            got = lax.dot_general(lhs, w, (((1,), (1,)), ((), ())), preferred_element_type=F32)
            acc = jnp.where(r256 == 2 * j + l256 // 128, got, acc)
        partial[pl.ds(start, 16), :] = jnp.where(row % 2 == 0, acc[:, :128], acc[:, 128:])
        return 0

    lax.fori_loop(0, 8, tiles, 0, unroll=2)

    part = partial[...]
    turned = pltpu.roll(part, 64, 1)
    low = iota((TILES, 128), 1) < 64
    stack = jnp.concatenate(
        [
            jnp.where(low, part, 0.0),
            jnp.where(low, turned, 0.0),
            jnp.where(low, 0.0, turned),
            jnp.where(low, 0.0, part),
        ],
        axis=0,
    )
    hi, lo = split(stack)
    slots = lax.dot_general(place[...], hi, (((1,), (0,)), ((), ())), preferred_element_type=F32)
    slots = slots + lax.dot_general(place[...], lo, (((1,), (0,)), ((), ())), preferred_element_type=F32)
    for p in range(2):
        vsend[pl.ds(p, PLANES, stride=3), 0, :] = slots[p * PLANES : (p + 1) * PLANES]
    pl.semaphore_wait(ready_sem, 15)
    spread()

    gathered()
    ids = vrecv[pl.ds(2, PLANES, stride=3), 0, :]
    group_lane = iota((PLANES, GRP_DEV), 1).astype(F32)
    hits = jnp.concatenate(
        [
            jnp.concatenate(
                [(ids[:, 2 * p + h : 2 * p + h + 1] == group_lane).astype(F32).astype(BF16) for h in range(2)], axis=1
            )
            for p in range(2)
        ],
        axis=0,
    )
    vals = jnp.concatenate([vrecv[pl.ds(p, PLANES, stride=3), 0, :] for p in range(2)], axis=0)
    hi, lo = split(vals)
    both = lax.dot_general(hi, hits, (((0,), (0,)), ((), ())), preferred_element_type=F32)
    both = both + lax.dot_general(lo, hits, (((0,), (0,)), ((), ())), preferred_element_type=F32)
    coef[...] = both[:KB, :GRP_DEV] + both[KB:, GRP_DEV:]
    last = pltpu.make_async_copy(coef, coef_out, out_sem.at[2])
    last.start()
    for c in outs:
        c.wait()
    for r, field in enumerate((p1, m1, p2, m2)):
        sent(r, field)
    all_sent()
    last.wait()


def local(
    electric_start,
    magnetic_start,
    current_start,
    cotangent,
    level_set,
    material,
    source_cell,
    basis,
    block_owner,
    block_group,
):
    field = (3, 16, 16, 128)
    brick = (16, 16, 128)
    anywhere = pl.BlockSpec(memory_space=pltpu.HBM)
    V, D = pltpu.VMEM, pltpu.SemaphoreType.DMA
    return pl.pallas_call(
        kernel,
        name="adjoint_step",
        out_shape=(
            jax.ShapeDtypeStruct(field, F32),
            jax.ShapeDtypeStruct(field, F32),
            jax.ShapeDtypeStruct((KB, GRP_DEV), F32),
        ),
        in_specs=[pl.BlockSpec(memory_space=pltpu.SMEM)] + [anywhere] * 9,
        out_specs=(anywhere,) * 3,
        scratch_shapes=[
            V((6, 17, 16, 128), F32),
            V((6, 17, 16, 128), F32),
            V((6, 17, 16, 128), F32),
            V((6, 17, 16, 128), F32),
            V(field, F32),
            V(field, F32),
            V(field, F32),
            V(brick, F32),
            V(brick, jnp.int32),
            V(brick, F32),
            V(brick, F32),
            V(brick, F32),
            V(brick, F32),
            V(field, F32),
            V(brick, F32),
            V((256, 128), F32),
            V(field, F32),
            V(field, F32),
            V((NB * KB, TILE), BF16),
            V((1, NB), jnp.int32),
            V((1, NB), jnp.int32),
            V((4, 4, 16, 128), F32),
            V((4, 4, 16, 128), F32),
            V((4, 16, 128), F32),
            V((4, 16, 128), F32),
            V((NB, 4 * TILES), BF16),
            V((TILES, 128), F32),
            V((3 * PLANES, 1, 128), F32),
            V((3 * PLANES, 1, 128), F32),
            V((KB, GRP_DEV), F32),
            D((10,)),
            D((NCHUNK,)),
            D((3,)),
            D((4, 3)),
            D((4, 3)),
            D((2,)),
            D,
            pltpu.SemaphoreType.REGULAR,
        ],
        compiler_params=pltpu.CompilerParams(
            collective_id=0, has_side_effects=True, vmem_limit_bytes=56000 << 10
        ),
    )(
        source_cell,
        electric_start,
        magnetic_start,
        current_start,
        cotangent,
        level_set,
        material,
        basis.reshape(NB * KB, TILE),
        block_owner.reshape(1, NB),
        block_group.reshape(1, NB),
    )


def solution(mesh):
    return jax.shard_map(
        local,
        mesh=mesh,
        in_specs=(
            P(None, "by", "bx", "gz"),
            P(None, "by", "bx", "gz"),
            P(None, "by", "bx", "gz"),
            P(None, "by", "bx", "gz"),
            P("by", "bx", "gz"),
            P("by", "bx", "gz"),
            P(("bx", "by", "gz")),
            P(("bx", "by", "gz"), None, None),
            P(("bx", "by", "gz"), None),
            P(("bx", "by", "gz")),
        ),
        out_specs=(
            P(None, "by", "bx", "gz"),
            P(None, "by", "bx", "gz"),
            P(None, ("bx", "by", "gz")),
        ),
        check_vma=False,
    )
```

```python
import jax
import jax.numpy as jnp
from jax import lax
from jax.experimental import pallas as pl
from jax.experimental.pallas import tpu as pltpu
from jax.sharding import PartitionSpec as P

KB = 64
GRP_DEV = 128
NBX = 4
NBY = 32
PLANES = 128
NB = 256
TILES = 128
TILE = 256
NCHUNK = 8

time_step = 0.5
drude_keep = 0.9
drude_gain = 1.0
metal_permit = 3.0
design_contrast = 5.0
source_level = 3.0
source_wave = (1.0, -0.6, 0.8, -0.4)

F32 = jnp.float32
BF16 = jnp.bfloat16
MESH = pl.DeviceIdType.MESH

IDX = {("x", 0): 0, ("z", 0): 1, ("y", 0): 2, ("x", 1): 3, ("z", 1): 4, ("y", 1): 5}
COMP = {"x": 0, "y": 1, "z": 2}


def iota(shape, dim):
    return lax.broadcasted_iota(jnp.int32, shape, dim)


def split(v):
    hi = v.astype(BF16)
    lo = (v - hi.astype(F32)).astype(BF16)
    return hi, lo


def kernel(
    source_ref,
    e0_hbm,
    h0_hbm,
    j0_hbm,
    cot_hbm,
    level_hbm,
    material_hbm,
    basis_hbm,
    owner_hbm,
    group_hbm,
    e_out,
    a_out,
    coef_out,
    p1,
    p2,
    m1,
    m2,
    h0,
    j0,
    cot,
    level,
    material,
    ratio,
    silver,
    factor,
    sources,
    adj1,
    drive1,
    part1,
    grad,
    efin,
    afin,
    basis,
    owner,
    group,
    xsend,
    xrecv,
    zsend,
    zrecv,
    place,
    partial,
    vsend,
    vrecv,
    coef,
    in_sem,
    basis_sem,
    out_sem,
    send_sem,
    recv_sem,
    a2a_sem,
    own_sem,
    ready_sem,
):
    bx, by, gz = lax.axis_index("bx"), lax.axis_index("by"), lax.axis_index("gz")
    me = bx * NBY + by
    yy, zz = by // 8, by % 8

    loads = [
        (material_hbm, material),
        (level_hbm, level),
        (cot_hbm, cot),
        (e0_hbm.at[0], p1.at[0, pl.ds(0, 16)]),
        (e0_hbm.at[2], p1.at[1, pl.ds(0, 16)]),
        (e0_hbm.at[1], p1.at[2, pl.ds(0, 16)]),
        (h0_hbm, h0),
        (j0_hbm, j0),
        (owner_hbm, owner),
        (group_hbm, group),
    ]
    loads = [pltpu.make_async_copy(s, d, in_sem.at[i]) for i, (s, d) in enumerate(loads)]
    for c in loads:
        c.start()

    zrow = jnp.zeros((2, 16, 128), F32)
    for ref, at in ((p1, 16), (p2, 16), (m1, 0), (m2, 0)):
        for t in range(2):
            ref[3 * t : 3 * t + 2, at] = zrow
    for r in range(4):
        for t in range(2):
            xrecv[r, t] = zrow
        zrecv[r] = zrow

    barrier = pltpu.get_barrier_semaphore()

    def hail(**where):
        pl.semaphore_signal(barrier, inc=1, device_id=where, device_id_type=MESH)

    for i in range(1, 8):
        hail(by=yy * 8 + (zz + i) % 8)
    for i in range(1, 4):
        hail(by=(yy + i) % 4 * 8 + zz)
        hail(bx=(bx + i) % 4)
    hail(gz=1 - gz)
    up_far = jnp.logical_and(zz == 7, by < NBY - 1)
    down_far = jnp.logical_and(zz == 0, by > 0)

    @pl.when(up_far)
    def _():
        hail(by=by + 1)

    @pl.when(down_far)
    def _():
        hail(by=by - 1)

    for c in loads[:6]:
        c.wait()
    bases = [
        pltpu.make_async_copy(
            basis_hbm.at[pl.ds(i * (NB * KB // NCHUNK), NB * KB // NCHUNK)],
            basis.at[pl.ds(i * (NB * KB // NCHUNK), NB * KB // NCHUNK)],
            basis_sem.at[i],
        )
        for i in range(NCHUNK)
    ]
    for c in bases:
        c.start()

    row = iota((16, 128), 0)
    lane = iota((16, 128), 1)

    def pack_z(acc, y, vals, from_lane):
        for c, v in enumerate(vals):
            at = 2 * y + c
            acc = jnp.where(lane == at, pltpu.roll(v, (at + 128 - from_lane) % 128, 1), acc)
        return acc

    def first(y, acc):
        mat = material[y]
        lev = level[y]
        smooth = jax.nn.sigmoid(lev)
        sil = (mat == 2).astype(F32)
        permit = jnp.where(mat == 2, metal_permit, jnp.where(mat == 1, 1.0 + design_contrast * smooth, 1.0))
        rat = time_step / permit
        ratio[y] = rat
        silver[y] = sil
        sx, sy, sz = (rat * cot[c, y] for c in range(3))
        p1[3, y] = sx
        p1[4, y] = sz
        p1[5, y] = sy
        ex, ey, ez = p1[0, y], p1[2, y], p1[1, y]
        for t, couple in enumerate(((ey, ez), (sy, sz))):
            for c, v in enumerate(couple):
                xsend[0, t, c, pl.ds(y, 1), :] = v[0:1]
        return pack_z(acc[0], y, (ex, ey), 0), pack_z(acc[1], y, (sx, sy), 0)

    empty = jnp.zeros((16, 128), F32)
    packs = lax.fori_loop(0, 16, first, (empty, empty), unroll=4)
    for t in range(2):
        zsend[0, t] = packs[t]

    pl.semaphore_wait(barrier, 14 + up_far.astype(jnp.int32) + down_far.astype(jnp.int32))
    for i in range(1, 4):
        pl.semaphore_signal(
            ready_sem.at[0], inc=1, device_id={"by": (yy + i) % 4 * 8 + zz}, device_id_type=MESH
        )

    def moves(r, t, field):
        plus = r % 2 == 0
        step = -1 if plus else 1
        edge, halo = (0, 16) if plus else (16, 0)

        def move(src, dst, i, **where):
            return pltpu.make_async_remote_copy(
                src_ref=src,
                dst_ref=dst,
                send_sem=send_sem.at[2 * r + t, i],
                recv_sem=recv_sem.at[2 * r + t, i],
                device_id=where,
                device_id_type=MESH,
            )

        y_out = by > 0 if plus else by < NBY - 1
        y_in = by < NBY - 1 if plus else by > 0
        x_out = bx > 0 if plus else bx < NBX - 1
        x_in = bx < NBX - 1 if plus else bx > 0
        z_out = gz == 1 if plus else gz == 0
        z_in = gz == 0 if plus else gz == 1
        return (
            (y_out, y_in, move(field.at[pl.ds(3 * t, 2), edge], field.at[pl.ds(3 * t, 2), halo], 0, by=by + step)),
            (x_out, x_in, move(xsend.at[r, t], xrecv.at[r, t], 1, bx=bx + step)),
            (z_out, z_in, move(zsend.at[r, t], zrecv.at[r, t], 2, gz=1 - gz)),
        )

    def send(r, t, field):
        for out, _, c in moves(r, t, field):
            pl.when(out)(c.start)

    def receive(r, t, field, first, last):
        for _, into, c in moves(r, t, field)[first:last]:
            pl.when(into)(c.wait_recv)

    def sent(r, t, field):
        for out, _, c in moves(r, t, field):
            pl.when(out)(c.wait_send)

    send(0, 0, p1)
    send(0, 1, p1)

    for c in loads[6:]:
        c.wait()

    def count(y, _):
        flat = y * 2048 + row * 128 + lane
        total = jnp.zeros((16, 128), F32)
        for i in range(8):
            total = total + (flat == source_ref[i]).astype(F32)
        sources[y] = total
        smooth = jax.nn.sigmoid(level[y])
        design = (material[y] == 1).astype(F32)
        factor[y] = -(design * design_contrast * (smooth * (1.0 - smooth))) * (ratio[y] * (1.0 / time_step))
        return 0

    lax.fori_loop(0, 16, count, 0, unroll=4)

    owner_row = owner[...].astype(F32)
    group_row = group[...].astype(F32)
    ri, ci = iota((NB, NB), 0), iota((NB, NB), 1)
    owner_wide = jnp.broadcast_to(owner_row, (NB, NB))
    owner_col = jnp.sum(jnp.where(ri == ci, owner_wide, 0.0), axis=1, keepdims=True)
    group_col = jnp.sum(jnp.where(ri == ci, jnp.broadcast_to(group_row, (NB, NB)), 0.0), axis=1, keepdims=True)
    same = jnp.logical_and(owner_wide == owner_col, ci < ri)
    rank_col = jnp.sum(same.astype(F32), axis=1, keepdims=True)
    target_col = owner_col * 4.0 + rank_col
    block, tile = iota((NB, TILES), 0), iota((NB, TILES), 1)
    id_sum = jnp.zeros((PLANES, 128), F32)
    dest, id_lane = iota((PLANES, TILES), 0), iota((PLANES, TILES), 1)
    targets, groups = [], []
    for f in range(2):
        pick = block == 2 * tile + f
        targets.append(jnp.sum(jnp.where(pick, target_col, 0.0), axis=0, keepdims=True))
        groups.append(jnp.sum(jnp.where(pick, group_col, 0.0), axis=0, keepdims=True))
    slot_row = (4 * (block % PLANES) + 2 * (block // PLANES)).astype(F32)
    for h in range(2):
        for f in range(2):
            place[:, pl.ds((2 * h + f) * TILES, TILES)] = (
                (targets[f] == slot_row + float(h)).astype(F32).astype(BF16)
            )
    first_slot = (4 * dest).astype(F32)
    for s in range(4):
        hit = jnp.zeros((PLANES, TILES), F32)
        for f in range(2):
            hit = hit + jnp.where(targets[f] == first_slot + float(s), groups[f], 0.0)
        id_sum = jnp.where(id_lane == s, jnp.sum(hit, axis=1, keepdims=True), id_sum)
    vsend[pl.ds(2, PLANES, stride=3), 0, :] = id_sum

    def plus_half(r, t, field, old, out):
        nxt = r + 1

        def body(y, acc):
            zf = zrecv[r, t]
            fx, fy, fz = (field[IDX[(c, t)], y] for c in "xyz")
            dyx = field[IDX[("x", t)], y + 1] - fx
            dyz = field[IDX[("z", t)], y + 1] - fz

            def along_x(v, c):
                return jnp.where(row == 15, xrecv[r, t, c, pl.ds(y, 1), :], pltpu.roll(v, 15, 0)) - v

            def along_z(v, c):
                return jnp.where(lane == 127, pltpu.roll(zf, 127 - 2 * y - c, 1), pltpu.roll(v, 127, 1)) - v

            dxy, dxz = along_x(fy, 0), along_x(fz, 1)
            dzx, dzy = along_z(fx, 0), along_z(fy, 1)
            turn = {"x": dyz - dzy, "y": dzx - dxz, "z": dxy - dyx}
            vals = {}
            for c in "xyz":
                vals[c] = old(t, c, y, turn[c])
                out[IDX[(c, t)], y + 1] = vals[c]
            for i, c in enumerate("yz"):
                xsend[nxt, t, i, pl.ds(y, 1), :] = vals[c][15:16]
            return pack_z(acc, y, (vals["x"], vals["y"]), 127)

        receive(r, t, field, 1, 3)
        acc = lax.fori_loop(0, 15, body, empty, unroll=5)
        receive(r, t, field, 0, 1)
        zsend[nxt, t] = body(15, acc)

    def minus_turn(r, t, field, y):
        zf = zrecv[r, t]
        fx, fy, fz = (field[IDX[(c, t)], y + 1] for c in "xyz")
        dyx = fx - field[IDX[("x", t)], y]
        dyz = fz - field[IDX[("z", t)], y]

        def along_x(v, c):
            return v - jnp.where(row == 0, xrecv[r, t, c, pl.ds(y, 1), :], pltpu.roll(v, 1, 0))

        def along_z(v, c):
            return v - jnp.where(lane == 0, pltpu.roll(zf, 128 - 2 * y - c, 1), pltpu.roll(v, 1, 1))

        dxy, dxz = along_x(fy, 0), along_x(fz, 1)
        dzx, dzy = along_z(fx, 0), along_z(fy, 1)
        return {"x": dyz - dzy, "y": dzx - dxz, "z": dxy - dyx}

    def old_first(s, c, y, turn):
        return turn if s else h0[COMP[c], y] - time_step * turn

    def old_second(s, c, y, turn):
        before = m1[IDX[(c, s)], y + 1]
        return before + turn if s else before - time_step * turn

    for t in range(2):
        plus_half(0, t, p1, old_first, m1)
        send(1, t, m1)

    pl.semaphore_wait(ready_sem.at[0], 3)
    for i in range(1, 4):
        pl.semaphore_signal(ready_sem.at[1], inc=1, device_id={"bx": (bx + i) % 4}, device_id_type=MESH)

    def chunk(p):
        return pl.ds(p * 3, 3)

    def mine():
        return pltpu.make_async_copy(vsend.at[chunk(me)], vrecv.at[chunk(me)], own_sem)

    def spread():
        def one(i, _):
            p = (me + i) % PLANES
            pltpu.make_async_remote_copy(
                src_ref=vsend.at[chunk(p)],
                dst_ref=vrecv.at[chunk(me)],
                send_sem=a2a_sem.at[0],
                recv_sem=a2a_sem.at[1],
                device_id={"bx": p // NBY, "by": p % NBY},
                device_id_type=MESH,
            ).start()
            return 0

        mine().start()
        lax.fori_loop(1, PLANES, one, 0, unroll=4)

    def gathered():
        many = pl.ds(0, (PLANES - 1) * 3)
        pltpu.make_async_copy(vrecv.at[many], vrecv.at[many], a2a_sem.at[1]).wait()
        mine().wait()

    def all_sent():
        many = pl.ds(0, (PLANES - 1) * 3)
        pltpu.make_async_copy(vsend.at[many], vsend.at[many], a2a_sem.at[0]).wait()

    def electric_first(y, acc):
        rat, sil = ratio[y], silver[y]
        turn = minus_turn(1, 0, m1, y)
        vals = {}
        for c in "xyz":
            e = p1[IDX[(c, 0)], y]
            cur = sil * (drude_keep * j0[COMP[c], y] + drude_gain * e)
            drive = turn[c] - cur
            j0[COMP[c], y] = cur
            drive1[COMP[c], y] = drive
            new = e + rat * drive
            if c == "z":
                new = new + source_level * source_wave[0] * sources[y]
            vals[c] = new
            p2[IDX[(c, 0)], y] = new
        for i, c in enumerate("yz"):
            xsend[2, 0, i, pl.ds(y, 1), :] = vals[c][0:1]
        return pack_z(acc, y, (vals["x"], vals["y"]), 0)

    def adjoint_first(y, acc):
        rat, sil = ratio[y], silver[y]
        back = minus_turn(1, 1, m1, y)
        total = jnp.zeros((16, 128), F32)
        vals = {}
        for c in "xyz":
            a = cot[COMP[c], y] - drude_gain * (sil * p1[IDX[(c, 1)], y]) - time_step * back[c]
            adj1[COMP[c], y] = a
            vals[c] = rat * a
            p2[IDX[(c, 1)], y] = vals[c]
            total = total + vals[c] * drive1[COMP[c], y]
        part1[y] = total
        for i, c in enumerate("yz"):
            xsend[2, 1, i, pl.ds(y, 1), :] = vals[c][0:1]
        return pack_z(acc, y, (vals["x"], vals["y"]), 0)

    for t, body in enumerate((electric_first, adjoint_first)):
        receive(1, t, m1, 1, 3)
        pack = lax.fori_loop(1, 16, body, empty, unroll=5)
        receive(1, t, m1, 0, 1)
        zsend[2, t] = body(0, pack)
        send(2, t, p2)
    for t in range(2):
        plus_half(2, t, p2, old_second, m2)
        send(3, t, m2)

    def drive_second(y, _):
        sil = silver[y]
        turn = minus_turn(3, 0, m2, y)
        total = part1[y]
        for c in "xyz":
            cur = sil * (drude_keep * j0[COMP[c], y] + drude_gain * p2[IDX[(c, 0)], y])
            drive = turn[c] - cur
            efin[COMP[c], y] = drive
            total = total + p1[IDX[(c, 1)], y] * drive
        grad[pl.ds(pl.multiple_of(y * 16, 16), 16), :] = factor[y] * total
        return 0

    receive(3, 0, m2, 1, 3)
    lax.fori_loop(1, 16, drive_second, 0, unroll=5)
    receive(3, 0, m2, 0, 1)
    drive_second(0, 0)
    for c in bases:
        c.wait()

    low128 = iota((16, 128), 1) < 64
    r256, l256 = iota((16, 256), 0), iota((16, 256), 1)

    def tiles(i, _):
        start = pl.multiple_of(i * 16, 16)
        even = grad[pl.ds(2 * start, 16, stride=2), :]
        odd = grad[pl.ds(2 * start + 1, 16, stride=2), :]
        lhs = jnp.concatenate([even.astype(BF16), odd.astype(BF16)], axis=1)
        acc = jnp.zeros((16, 256), F32)
        for j in range(8):
            w = basis[pl.ds(pl.multiple_of(i * 2048 + j * 256, 256), 256), :]
            got = lax.dot_general(lhs, w, (((1,), (1,)), ((), ())), preferred_element_type=F32)
            acc = jnp.where(r256 == 2 * j + l256 // 128, got, acc)
        partial[pl.ds(start, 16), :] = jnp.where(row % 2 == 0, acc[:, :128], acc[:, 128:])
        return 0

    lax.fori_loop(0, 8, tiles, 0, unroll=4)

    part = partial[...]
    turned = pltpu.roll(part, 64, 1)
    low = iota((TILES, 128), 1) < 64
    stack = jnp.concatenate(
        [
            jnp.where(low, part, 0.0),
            jnp.where(low, turned, 0.0),
            jnp.where(low, 0.0, turned),
            jnp.where(low, 0.0, part),
        ],
        axis=0,
    )
    hi, lo = split(stack)
    slots = lax.dot_general(place[...], hi, (((1,), (0,)), ((), ())), preferred_element_type=F32)
    slots = slots + lax.dot_general(place[...], lo, (((1,), (0,)), ((), ())), preferred_element_type=F32)
    for p in range(2):
        vsend[pl.ds(p, PLANES, stride=3), 0, :] = slots[p * PLANES : (p + 1) * PLANES]
    pl.semaphore_wait(ready_sem.at[1], 3)
    spread()

    def fields(y, _):
        rat, sil = ratio[y], silver[y]
        back = minus_turn(3, 1, m2, y)
        for c in "xyz":
            new = p2[IDX[(c, 0)], y] + rat * efin[COMP[c], y]
            if c == "z":
                new = new + source_level * source_wave[1] * sources[y]
            efin[COMP[c], y] = new
            adj_drive = -drude_keep * (sil * p1[IDX[(c, 1)], y]) - p2[IDX[(c, 1)], y]
            afin[COMP[c], y] = adj1[COMP[c], y] + drude_gain * (sil * adj_drive) - time_step * back[c]
        return 0

    receive(3, 1, m2, 0, 3)
    lax.fori_loop(0, 16, fields, 0, unroll=4)
    outs = [
        pltpu.make_async_copy(efin, e_out, out_sem.at[0]),
        pltpu.make_async_copy(afin, a_out, out_sem.at[1]),
    ]
    for c in outs:
        c.start()

    gathered()
    ids = vrecv[pl.ds(2, PLANES, stride=3), 0, :]
    group_lane = iota((PLANES, GRP_DEV), 1).astype(F32)
    hits = jnp.concatenate(
        [
            jnp.concatenate(
                [(ids[:, 2 * p + h : 2 * p + h + 1] == group_lane).astype(F32).astype(BF16) for h in range(2)], axis=1
            )
            for p in range(2)
        ],
        axis=0,
    )
    vals = jnp.concatenate([vrecv[pl.ds(p, PLANES, stride=3), 0, :] for p in range(2)], axis=0)
    hi, lo = split(vals)
    both = lax.dot_general(hi, hits, (((0,), (0,)), ((), ())), preferred_element_type=F32)
    both = both + lax.dot_general(lo, hits, (((0,), (0,)), ((), ())), preferred_element_type=F32)
    coef[...] = both[:KB, :GRP_DEV] + both[KB:, GRP_DEV:]
    last = pltpu.make_async_copy(coef, coef_out, out_sem.at[2])
    last.start()
    for c in outs:
        c.wait()
    for r, field in enumerate((p1, m1, p2, m2)):
        for t in range(2):
            sent(r, t, field)
    all_sent()
    last.wait()


def local(
    electric_start,
    magnetic_start,
    current_start,
    cotangent,
    level_set,
    material,
    source_cell,
    basis,
    block_owner,
    block_group,
):
    field = (3, 16, 16, 128)
    brick = (16, 16, 128)
    anywhere = pl.BlockSpec(memory_space=pltpu.HBM)
    V, D = pltpu.VMEM, pltpu.SemaphoreType.DMA
    return pl.pallas_call(
        kernel,
        name="adjoint_step",
        out_shape=(
            jax.ShapeDtypeStruct(field, F32),
            jax.ShapeDtypeStruct(field, F32),
            jax.ShapeDtypeStruct((KB, GRP_DEV), F32),
        ),
        in_specs=[pl.BlockSpec(memory_space=pltpu.SMEM)] + [anywhere] * 9,
        out_specs=(anywhere,) * 3,
        scratch_shapes=[
            V((6, 17, 16, 128), F32),
            V((6, 17, 16, 128), F32),
            V((6, 17, 16, 128), F32),
            V((6, 17, 16, 128), F32),
            V(field, F32),
            V(field, F32),
            V(field, F32),
            V(brick, F32),
            V(brick, jnp.int32),
            V(brick, F32),
            V(brick, F32),
            V(brick, F32),
            V(brick, F32),
            V(field, F32),
            V(field, F32),
            V(brick, F32),
            V((256, 128), F32),
            V(field, F32),
            V(field, F32),
            V((NB * KB, TILE), BF16),
            V((1, NB), jnp.int32),
            V((1, NB), jnp.int32),
            V((4, 2, 2, 16, 128), F32),
            V((4, 2, 2, 16, 128), F32),
            V((4, 2, 16, 128), F32),
            V((4, 2, 16, 128), F32),
            V((NB, 4 * TILES), BF16),
            V((TILES, 128), F32),
            V((3 * PLANES, 1, 128), F32),
            V((3 * PLANES, 1, 128), F32),
            V((KB, GRP_DEV), F32),
            D((10,)),
            D((NCHUNK,)),
            D((3,)),
            D((8, 3)),
            D((8, 3)),
            D((2,)),
            D,
            pltpu.SemaphoreType.REGULAR((2,)),
        ],
        compiler_params=pltpu.CompilerParams(
            collective_id=0, has_side_effects=True, vmem_limit_bytes=56000 << 10
        ),
    )(
        source_cell,
        electric_start,
        magnetic_start,
        current_start,
        cotangent,
        level_set,
        material,
        basis.reshape(NB * KB, TILE),
        block_owner.reshape(1, NB),
        block_group.reshape(1, NB),
    )


def solution(mesh):
    return jax.shard_map(
        local,
        mesh=mesh,
        in_specs=(
            P(None, "by", "bx", "gz"),
            P(None, "by", "bx", "gz"),
            P(None, "by", "bx", "gz"),
            P(None, "by", "bx", "gz"),
            P("by", "bx", "gz"),
            P("by", "bx", "gz"),
            P(("bx", "by", "gz")),
            P(("bx", "by", "gz"), None, None),
            P(("bx", "by", "gz"), None),
            P(("bx", "by", "gz")),
        ),
        out_specs=(
            P(None, "by", "bx", "gz"),
            P(None, "by", "bx", "gz"),
            P(None, ("bx", "by", "gz")),
        ),
        check_vma=False,
    )
```

```python
import jax
import jax.numpy as jnp
from jax import lax
from jax.experimental import pallas as pl
from jax.experimental.pallas import tpu as pltpu
from jax.sharding import PartitionSpec as P

KB = 64
GRP_DEV = 128
NBX = 4
NBY = 32
PLANES = 128
NB = 256
TILES = 128
TILE = 256
NCHUNK = 8

time_step = 0.5
drude_keep = 0.9
drude_gain = 1.0
metal_permit = 3.0
design_contrast = 5.0
source_level = 3.0
source_wave = (1.0, -0.6, 0.8, -0.4)

F32 = jnp.float32
BF16 = jnp.bfloat16
MESH = pl.DeviceIdType.MESH

IDX = {("x", 0): 0, ("z", 0): 1, ("y", 0): 2, ("x", 1): 3, ("z", 1): 4, ("y", 1): 5}
COMP = {"x": 0, "y": 1, "z": 2}


def iota(shape, dim):
    return lax.broadcasted_iota(jnp.int32, shape, dim)


def split(v):
    hi = v.astype(BF16)
    lo = (v - hi.astype(F32)).astype(BF16)
    return hi, lo


def kernel(
    source_ref,
    e0_hbm,
    h0_hbm,
    j0_hbm,
    cot_hbm,
    level_hbm,
    material_hbm,
    basis_hbm,
    owner_hbm,
    group_hbm,
    e_out,
    a_out,
    coef_out,
    p1,
    p2,
    m1,
    m2,
    h0,
    j0,
    cot,
    level,
    material,
    ratio,
    silver,
    factor,
    sources,
    adj1,
    drive1,
    part1,
    grad,
    basis,
    owner,
    group,
    xsend,
    xrecv,
    zsend,
    zrecv,
    place,
    partial,
    vsend,
    vrecv,
    in_sem,
    basis_sem,
    send_sem,
    recv_sem,
    a2a_sem,
    own_sem,
    ready_sem,
):
    bx, by, gz = lax.axis_index("bx"), lax.axis_index("by"), lax.axis_index("gz")
    me = bx * NBY + by
    yy, zz = by // 8, by % 8

    loads = [
        (material_hbm, material),
        (level_hbm, level),
        (cot_hbm, cot),
        (e0_hbm.at[0], p1.at[0, pl.ds(0, 16)]),
        (e0_hbm.at[2], p1.at[1, pl.ds(0, 16)]),
        (e0_hbm.at[1], p1.at[2, pl.ds(0, 16)]),
        (h0_hbm, h0),
        (j0_hbm, j0),
        (owner_hbm, owner),
        (group_hbm, group),
    ]
    loads = [pltpu.make_async_copy(s, d, in_sem.at[i]) for i, (s, d) in enumerate(loads)]
    for c in loads:
        c.start()

    zrow = jnp.zeros((2, 16, 128), F32)
    for ref, at in ((p1, 16), (p2, 16), (m1, 0), (m2, 0)):
        for t in range(2):
            ref[3 * t : 3 * t + 2, at] = zrow
    for r in range(4):
        for t in range(2):
            xrecv[r, t] = zrow
        zrecv[r] = zrow

    barrier = pltpu.get_barrier_semaphore()

    def hail(**where):
        pl.semaphore_signal(barrier, inc=1, device_id=where, device_id_type=MESH)

    for i in range(1, 8):
        hail(by=yy * 8 + (zz + i) % 8)
    for i in range(1, 4):
        hail(by=(yy + i) % 4 * 8 + zz)
        hail(bx=(bx + i) % 4)
    hail(gz=1 - gz)
    up_far = jnp.logical_and(zz == 7, by < NBY - 1)
    down_far = jnp.logical_and(zz == 0, by > 0)

    @pl.when(up_far)
    def _():
        hail(by=by + 1)

    @pl.when(down_far)
    def _():
        hail(by=by - 1)

    for c in loads[:6]:
        c.wait()
    bases = [
        pltpu.make_async_copy(
            basis_hbm.at[pl.ds(i * (NB * KB // NCHUNK), NB * KB // NCHUNK)],
            basis.at[pl.ds(i * (NB * KB // NCHUNK), NB * KB // NCHUNK)],
            basis_sem.at[i],
        )
        for i in range(NCHUNK)
    ]
    for c in bases:
        c.start()

    row = iota((16, 128), 0)
    lane = iota((16, 128), 1)

    def pack_z(acc, y, vals, from_lane):
        for c, v in enumerate(vals):
            at = 2 * y + c
            acc = jnp.where(lane == at, pltpu.roll(v, (at + 128 - from_lane) % 128, 1), acc)
        return acc

    def first(y, acc):
        mat = material[y]
        lev = level[y]
        smooth = jax.nn.sigmoid(lev)
        sil = (mat == 2).astype(F32)
        permit = jnp.where(mat == 2, metal_permit, jnp.where(mat == 1, 1.0 + design_contrast * smooth, 1.0))
        rat = time_step / permit
        ratio[y] = rat
        silver[y] = sil
        sx, sy, sz = (rat * cot[c, y] for c in range(3))
        p1[3, y] = sx
        p1[4, y] = sz
        p1[5, y] = sy
        ex, ey, ez = p1[0, y], p1[2, y], p1[1, y]
        for t, couple in enumerate(((ey, ez), (sy, sz))):
            for c, v in enumerate(couple):
                xsend[0, t, c, pl.ds(y, 1), :] = v[0:1]
        return pack_z(acc[0], y, (ex, ey), 0), pack_z(acc[1], y, (sx, sy), 0)

    empty = jnp.zeros((16, 128), F32)
    packs = lax.fori_loop(0, 16, first, (empty, empty), unroll=4)
    for t in range(2):
        zsend[0, t] = packs[t]

    pl.semaphore_wait(barrier, 14 + up_far.astype(jnp.int32) + down_far.astype(jnp.int32))
    for i in range(1, 4):
        pl.semaphore_signal(
            ready_sem.at[0], inc=1, device_id={"by": (yy + i) % 4 * 8 + zz}, device_id_type=MESH
        )

    def moves(r, t, field):
        plus = r % 2 == 0
        step = -1 if plus else 1
        edge, halo = (0, 16) if plus else (16, 0)

        def move(src, dst, i, **where):
            return pltpu.make_async_remote_copy(
                src_ref=src,
                dst_ref=dst,
                send_sem=send_sem.at[2 * r + t, i],
                recv_sem=recv_sem.at[2 * r + t, i],
                device_id=where,
                device_id_type=MESH,
            )

        y_out = by > 0 if plus else by < NBY - 1
        y_in = by < NBY - 1 if plus else by > 0
        x_out = bx > 0 if plus else bx < NBX - 1
        x_in = bx < NBX - 1 if plus else bx > 0
        z_out = gz == 1 if plus else gz == 0
        z_in = gz == 0 if plus else gz == 1
        return (
            (y_out, y_in, move(field.at[pl.ds(3 * t, 2), edge], field.at[pl.ds(3 * t, 2), halo], 0, by=by + step)),
            (x_out, x_in, move(xsend.at[r, t], xrecv.at[r, t], 1, bx=bx + step)),
            (z_out, z_in, move(zsend.at[r, t], zrecv.at[r, t], 2, gz=1 - gz)),
        )

    def send(r, t, field):
        for out, _, c in moves(r, t, field):
            pl.when(out)(c.start)

    def receive(r, t, field, first, last):
        for _, into, c in moves(r, t, field)[first:last]:
            pl.when(into)(c.wait_recv)

    def sent(r, t, field):
        for out, _, c in moves(r, t, field):
            pl.when(out)(c.wait_send)

    send(0, 0, p1)
    send(0, 1, p1)

    for c in loads[6:]:
        c.wait()

    def count(y, _):
        flat = y * 2048 + row * 128 + lane
        total = jnp.zeros((16, 128), F32)
        for i in range(8):
            total = total + (flat == source_ref[i]).astype(F32)
        sources[y] = total
        smooth = jax.nn.sigmoid(level[y])
        design = (material[y] == 1).astype(F32)
        factor[y] = -(design * design_contrast * (smooth * (1.0 - smooth))) * (ratio[y] * (1.0 / time_step))
        return 0

    lax.fori_loop(0, 16, count, 0, unroll=4)

    owner_row = owner[...].astype(F32)
    group_row = group[...].astype(F32)
    ri, ci = iota((NB, NB), 0), iota((NB, NB), 1)
    owner_wide = jnp.broadcast_to(owner_row, (NB, NB))
    owner_col = jnp.sum(jnp.where(ri == ci, owner_wide, 0.0), axis=1, keepdims=True)
    group_col = jnp.sum(jnp.where(ri == ci, jnp.broadcast_to(group_row, (NB, NB)), 0.0), axis=1, keepdims=True)
    same = jnp.logical_and(owner_wide == owner_col, ci < ri)
    rank_col = jnp.sum(same.astype(F32), axis=1, keepdims=True)
    target_col = owner_col * 4.0 + rank_col
    block, tile = iota((NB, TILES), 0), iota((NB, TILES), 1)
    id_sum = jnp.zeros((PLANES, 128), F32)
    dest, id_lane = iota((PLANES, TILES), 0), iota((PLANES, TILES), 1)
    targets, groups = [], []
    for f in range(2):
        pick = block == 2 * tile + f
        targets.append(jnp.sum(jnp.where(pick, target_col, 0.0), axis=0, keepdims=True))
        groups.append(jnp.sum(jnp.where(pick, group_col, 0.0), axis=0, keepdims=True))
    slot_row = (4 * (block % PLANES) + 2 * (block // PLANES)).astype(F32)
    for h in range(2):
        for f in range(2):
            place[:, pl.ds((2 * h + f) * TILES, TILES)] = (
                (targets[f] == slot_row + float(h)).astype(F32).astype(BF16)
            )
    first_slot = (4 * dest).astype(F32)
    for s in range(4):
        hit = jnp.zeros((PLANES, TILES), F32)
        for f in range(2):
            hit = hit + jnp.where(targets[f] == first_slot + float(s), groups[f], 0.0)
        id_sum = jnp.where(id_lane == s, jnp.sum(hit, axis=1, keepdims=True), id_sum)
    vsend[pl.ds(2, PLANES, stride=3), 0, :] = id_sum

    def plus_half(r, t, field, old, out):
        nxt = r + 1

        def body(y, acc):
            zf = zrecv[r, t]
            fx, fy, fz = (field[IDX[(c, t)], y] for c in "xyz")
            dyx = field[IDX[("x", t)], y + 1] - fx
            dyz = field[IDX[("z", t)], y + 1] - fz

            def along_x(v, c):
                return jnp.where(row == 15, xrecv[r, t, c, pl.ds(y, 1), :], pltpu.roll(v, 15, 0)) - v

            def along_z(v, c):
                return jnp.where(lane == 127, pltpu.roll(zf, 127 - 2 * y - c, 1), pltpu.roll(v, 127, 1)) - v

            dxy, dxz = along_x(fy, 0), along_x(fz, 1)
            dzx, dzy = along_z(fx, 0), along_z(fy, 1)
            turn = {"x": dyz - dzy, "y": dzx - dxz, "z": dxy - dyx}
            vals = {}
            for c in "xyz":
                vals[c] = old(t, c, y, turn[c])
                out[IDX[(c, t)], y + 1] = vals[c]
            for i, c in enumerate("yz"):
                xsend[nxt, t, i, pl.ds(y, 1), :] = vals[c][15:16]
            return pack_z(acc, y, (vals["x"], vals["y"]), 127)

        receive(r, t, field, 1, 3)
        acc = lax.fori_loop(0, 15, body, empty, unroll=5)
        receive(r, t, field, 0, 1)
        zsend[nxt, t] = body(15, acc)

    def minus_turn(r, t, field, y):
        zf = zrecv[r, t]
        fx, fy, fz = (field[IDX[(c, t)], y + 1] for c in "xyz")
        dyx = fx - field[IDX[("x", t)], y]
        dyz = fz - field[IDX[("z", t)], y]

        def along_x(v, c):
            return v - jnp.where(row == 0, xrecv[r, t, c, pl.ds(y, 1), :], pltpu.roll(v, 1, 0))

        def along_z(v, c):
            return v - jnp.where(lane == 0, pltpu.roll(zf, 128 - 2 * y - c, 1), pltpu.roll(v, 1, 1))

        dxy, dxz = along_x(fy, 0), along_x(fz, 1)
        dzx, dzy = along_z(fx, 0), along_z(fy, 1)
        return {"x": dyz - dzy, "y": dzx - dxz, "z": dxy - dyx}

    def old_first(s, c, y, turn):
        return turn if s else h0[COMP[c], y] - time_step * turn

    def old_second(s, c, y, turn):
        before = m1[IDX[(c, s)], y + 1]
        return before + turn if s else before - time_step * turn

    for t in range(2):
        plus_half(0, t, p1, old_first, m1)
        send(1, t, m1)

    pl.semaphore_wait(ready_sem.at[0], 3)
    for i in range(1, 4):
        pl.semaphore_signal(ready_sem.at[1], inc=1, device_id={"bx": (bx + i) % 4}, device_id_type=MESH)

    def chunk(p):
        return pl.ds(p * 3, 3)

    def mine():
        return pltpu.make_async_copy(vsend.at[chunk(me)], vrecv.at[chunk(me)], own_sem)

    def spread():
        def one(i, _):
            p = (me + i) % PLANES
            pltpu.make_async_remote_copy(
                src_ref=vsend.at[chunk(p)],
                dst_ref=vrecv.at[chunk(me)],
                send_sem=a2a_sem.at[0],
                recv_sem=a2a_sem.at[1],
                device_id={"bx": p // NBY, "by": p % NBY},
                device_id_type=MESH,
            ).start()
            return 0

        mine().start()
        lax.fori_loop(1, PLANES, one, 0, unroll=4)

    def gathered():
        many = pl.ds(0, (PLANES - 1) * 3)
        pltpu.make_async_copy(vrecv.at[many], vrecv.at[many], a2a_sem.at[1]).wait()
        mine().wait()

    def all_sent():
        many = pl.ds(0, (PLANES - 1) * 3)
        pltpu.make_async_copy(vsend.at[many], vsend.at[many], a2a_sem.at[0]).wait()

    def electric_first(y, acc):
        rat, sil = ratio[y], silver[y]
        turn = minus_turn(1, 0, m1, y)
        vals = {}
        for c in "xyz":
            e = p1[IDX[(c, 0)], y]
            cur = sil * (drude_keep * j0[COMP[c], y] + drude_gain * e)
            drive = turn[c] - cur
            j0[COMP[c], y] = cur
            drive1[COMP[c], y] = drive
            new = e + rat * drive
            if c == "z":
                new = new + source_level * source_wave[0] * sources[y]
            vals[c] = new
            p2[IDX[(c, 0)], y] = new
        for i, c in enumerate("yz"):
            xsend[2, 0, i, pl.ds(y, 1), :] = vals[c][0:1]
        return pack_z(acc, y, (vals["x"], vals["y"]), 0)

    def adjoint_first(y, acc):
        rat, sil = ratio[y], silver[y]
        back = minus_turn(1, 1, m1, y)
        total = jnp.zeros((16, 128), F32)
        vals = {}
        for c in "xyz":
            a = cot[COMP[c], y] - drude_gain * (sil * p1[IDX[(c, 1)], y]) - time_step * back[c]
            adj1[COMP[c], y] = a
            vals[c] = rat * a
            p2[IDX[(c, 1)], y] = vals[c]
            total = total + vals[c] * drive1[COMP[c], y]
        part1[y] = total
        for i, c in enumerate("yz"):
            xsend[2, 1, i, pl.ds(y, 1), :] = vals[c][0:1]
        return pack_z(acc, y, (vals["x"], vals["y"]), 0)

    for t, body in enumerate((electric_first, adjoint_first)):
        receive(1, t, m1, 1, 3)
        pack = lax.fori_loop(1, 16, body, empty, unroll=5)
        receive(1, t, m1, 0, 1)
        zsend[2, t] = body(0, pack)
        send(2, t, p2)
    for t in range(2):
        plus_half(2, t, p2, old_second, m2)
        send(3, t, m2)

    def drive_second(y, _):
        sil = silver[y]
        turn = minus_turn(3, 0, m2, y)
        total = part1[y]
        for c in "xyz":
            cur = sil * (drude_keep * j0[COMP[c], y] + drude_gain * p2[IDX[(c, 0)], y])
            drive = turn[c] - cur
            e_out[COMP[c], y] = drive
            total = total + p1[IDX[(c, 1)], y] * drive
        grad[pl.ds(pl.multiple_of(y * 16, 16), 16), :] = factor[y] * total
        return 0

    receive(3, 0, m2, 1, 3)
    lax.fori_loop(1, 16, drive_second, 0, unroll=5)
    receive(3, 0, m2, 0, 1)
    drive_second(0, 0)
    for c in bases:
        c.wait()

    low128 = iota((16, 128), 1) < 64
    r256, l256 = iota((16, 256), 0), iota((16, 256), 1)

    def tiles(i, _):
        start = pl.multiple_of(i * 16, 16)
        even = grad[pl.ds(2 * start, 16, stride=2), :]
        odd = grad[pl.ds(2 * start + 1, 16, stride=2), :]
        lhs = jnp.concatenate([even.astype(BF16), odd.astype(BF16)], axis=1)
        acc = jnp.zeros((16, 256), F32)
        for j in range(8):
            w = basis[pl.ds(pl.multiple_of(i * 2048 + j * 256, 256), 256), :]
            got = lax.dot_general(lhs, w, (((1,), (1,)), ((), ())), preferred_element_type=F32)
            acc = jnp.where(r256 == 2 * j + l256 // 128, got, acc)
        partial[pl.ds(start, 16), :] = jnp.where(row % 2 == 0, acc[:, :128], acc[:, 128:])
        return 0

    lax.fori_loop(0, 8, tiles, 0, unroll=4)

    part = partial[...]
    turned = pltpu.roll(part, 64, 1)
    low = iota((TILES, 128), 1) < 64
    stack = jnp.concatenate(
        [
            jnp.where(low, part, 0.0),
            jnp.where(low, turned, 0.0),
            jnp.where(low, 0.0, turned),
            jnp.where(low, 0.0, part),
        ],
        axis=0,
    )
    hi, lo = split(stack)
    slots = lax.dot_general(place[...], hi, (((1,), (0,)), ((), ())), preferred_element_type=F32)
    slots = slots + lax.dot_general(place[...], lo, (((1,), (0,)), ((), ())), preferred_element_type=F32)
    for p in range(2):
        vsend[pl.ds(p, PLANES, stride=3), 0, :] = slots[p * PLANES : (p + 1) * PLANES]
    pl.semaphore_wait(ready_sem.at[1], 3)
    spread()

    def fields(y, _):
        rat, sil = ratio[y], silver[y]
        back = minus_turn(3, 1, m2, y)
        for c in "xyz":
            new = p2[IDX[(c, 0)], y] + rat * e_out[COMP[c], y]
            if c == "z":
                new = new + source_level * source_wave[1] * sources[y]
            e_out[COMP[c], y] = new
            adj_drive = -drude_keep * (sil * p1[IDX[(c, 1)], y]) - p2[IDX[(c, 1)], y]
            a_out[COMP[c], y] = adj1[COMP[c], y] + drude_gain * (sil * adj_drive) - time_step * back[c]
        return 0

    receive(3, 1, m2, 0, 3)
    lax.fori_loop(0, 16, fields, 0, unroll=4)

    gathered()
    ids = vrecv[pl.ds(2, PLANES, stride=3), 0, :]
    group_lane = iota((PLANES, GRP_DEV), 1).astype(F32)
    hits = jnp.concatenate(
        [
            jnp.concatenate(
                [(ids[:, 2 * p + h : 2 * p + h + 1] == group_lane).astype(F32).astype(BF16) for h in range(2)], axis=1
            )
            for p in range(2)
        ],
        axis=0,
    )
    vals = jnp.concatenate([vrecv[pl.ds(p, PLANES, stride=3), 0, :] for p in range(2)], axis=0)
    hi, lo = split(vals)
    both = lax.dot_general(hi, hits, (((0,), (0,)), ((), ())), preferred_element_type=F32)
    both = both + lax.dot_general(lo, hits, (((0,), (0,)), ((), ())), preferred_element_type=F32)
    coef_out[...] = both[:KB, :GRP_DEV] + both[KB:, GRP_DEV:]
    for r, field in enumerate((p1, m1, p2, m2)):
        for t in range(2):
            sent(r, t, field)
    all_sent()


def local(
    electric_start,
    magnetic_start,
    current_start,
    cotangent,
    level_set,
    material,
    source_cell,
    basis,
    block_owner,
    block_group,
):
    field = (3, 16, 16, 128)
    brick = (16, 16, 128)
    anywhere = pl.BlockSpec(memory_space=pltpu.HBM)
    V, D = pltpu.VMEM, pltpu.SemaphoreType.DMA
    return pl.pallas_call(
        kernel,
        name="adjoint_step",
        out_shape=(
            V(field, F32),
            V(field, F32),
            V((KB, GRP_DEV), F32),
        ),
        in_specs=[pl.BlockSpec(memory_space=pltpu.SMEM)] + [anywhere] * 9,
        out_specs=(pl.BlockSpec(memory_space=pltpu.VMEM),) * 3,
        scratch_shapes=[
            V((6, 17, 16, 128), F32),
            V((6, 17, 16, 128), F32),
            V((6, 17, 16, 128), F32),
            V((6, 17, 16, 128), F32),
            V(field, F32),
            V(field, F32),
            V(field, F32),
            V(brick, F32),
            V(brick, jnp.int32),
            V(brick, F32),
            V(brick, F32),
            V(brick, F32),
            V(brick, F32),
            V(field, F32),
            V(field, F32),
            V(brick, F32),
            V((256, 128), F32),
            V((NB * KB, TILE), BF16),
            V((1, NB), jnp.int32),
            V((1, NB), jnp.int32),
            V((4, 2, 2, 16, 128), F32),
            V((4, 2, 2, 16, 128), F32),
            V((4, 2, 16, 128), F32),
            V((4, 2, 16, 128), F32),
            V((NB, 4 * TILES), BF16),
            V((TILES, 128), F32),
            V((3 * PLANES, 1, 128), F32),
            V((3 * PLANES, 1, 128), F32),
            D((10,)),
            D((NCHUNK,)),
            D((8, 3)),
            D((8, 3)),
            D((2,)),
            D,
            pltpu.SemaphoreType.REGULAR((2,)),
        ],
        compiler_params=pltpu.CompilerParams(
            collective_id=0, has_side_effects=True, vmem_limit_bytes=56000 << 10
        ),
    )(
        source_cell,
        electric_start,
        magnetic_start,
        current_start,
        cotangent,
        level_set,
        material,
        basis.reshape(NB * KB, TILE),
        block_owner.reshape(1, NB),
        block_group.reshape(1, NB),
    )


def solution(mesh):
    return jax.shard_map(
        local,
        mesh=mesh,
        in_specs=(
            P(None, "by", "bx", "gz"),
            P(None, "by", "bx", "gz"),
            P(None, "by", "bx", "gz"),
            P(None, "by", "bx", "gz"),
            P("by", "bx", "gz"),
            P("by", "bx", "gz"),
            P(("bx", "by", "gz")),
            P(("bx", "by", "gz"), None, None),
            P(("bx", "by", "gz"), None),
            P(("bx", "by", "gz")),
        ),
        out_specs=(
            P(None, "by", "bx", "gz"),
            P(None, "by", "bx", "gz"),
            P(None, ("bx", "by", "gz")),
        ),
        check_vma=False,
    )
```

```python
import jax
import jax.numpy as jnp
from jax import lax
from jax.experimental import pallas as pl
from jax.experimental.pallas import tpu as pltpu
from jax.sharding import PartitionSpec as P

KB = 64
GRP_DEV = 128
NBX = 4
NBY = 32
PLANES = 128
NB = 256
TILES = 128
TILE = 256
NCHUNK = 8

time_step = 0.5
drude_keep = 0.9
drude_gain = 1.0
metal_permit = 3.0
design_contrast = 5.0
source_level = 3.0
source_wave = (1.0, -0.6, 0.8, -0.4)

F32 = jnp.float32
BF16 = jnp.bfloat16
MESH = pl.DeviceIdType.MESH

IDX = {("x", 0): 0, ("z", 0): 1, ("y", 0): 2, ("x", 1): 3, ("z", 1): 4, ("y", 1): 5}
COMP = {"x": 0, "y": 1, "z": 2}


def iota(shape, dim):
    return lax.broadcasted_iota(jnp.int32, shape, dim)


def split(v):
    hi = v.astype(BF16)
    lo = (v - hi.astype(F32)).astype(BF16)
    return hi, lo


def kernel(
    source_ref,
    e0_hbm,
    h0_hbm,
    j0_hbm,
    cot_hbm,
    level_hbm,
    material_hbm,
    basis_hbm,
    owner_hbm,
    group_hbm,
    e_out,
    a_out,
    coef_out,
    p1,
    p2,
    m1,
    m2,
    h0,
    j0,
    cot,
    level,
    material,
    ratio,
    silver,
    factor,
    sources,
    adj1,
    drive1,
    part1,
    grad,
    basis,
    owner,
    group,
    xsend,
    xrecv,
    zsend,
    zrecv,
    place,
    partial,
    vsend,
    vrecv,
    in_sem,
    basis_sem,
    send_sem,
    recv_sem,
    a2a_sem,
    own_sem,
    ready_sem,
):
    bx, by, gz = lax.axis_index("bx"), lax.axis_index("by"), lax.axis_index("gz")
    me = bx * NBY + by
    yy, zz = by // 8, by % 8

    loads = [
        (material_hbm, material),
        (level_hbm, level),
        (cot_hbm, cot),
        (e0_hbm.at[0], p1.at[0, pl.ds(0, 16)]),
        (e0_hbm.at[2], p1.at[1, pl.ds(0, 16)]),
        (e0_hbm.at[1], p1.at[2, pl.ds(0, 16)]),
        (h0_hbm, h0),
        (j0_hbm, j0),
        (owner_hbm, owner),
        (group_hbm, group),
    ]
    loads = [pltpu.make_async_copy(s, d, in_sem.at[i]) for i, (s, d) in enumerate(loads)]
    for c in loads:
        c.start()

    zrow = jnp.zeros((2, 16, 128), F32)
    for ref, at in ((p1, 16), (p2, 16), (m1, 0), (m2, 0)):
        for t in range(2):
            ref[3 * t : 3 * t + 2, at] = zrow
    for r in range(4):
        for t in range(2):
            xrecv[r, t] = zrow
        zrecv[r] = zrow

    barrier = pltpu.get_barrier_semaphore()

    def hail(**where):
        pl.semaphore_signal(barrier, inc=1, device_id=where, device_id_type=MESH)

    for i in range(1, 8):
        hail(by=yy * 8 + (zz + i) % 8)
    for i in range(1, 4):
        hail(by=(yy + i) % 4 * 8 + zz)
        hail(bx=(bx + i) % 4)
    hail(gz=1 - gz)
    up_far = jnp.logical_and(zz == 7, by < NBY - 1)
    down_far = jnp.logical_and(zz == 0, by > 0)

    @pl.when(up_far)
    def _():
        hail(by=by + 1)

    @pl.when(down_far)
    def _():
        hail(by=by - 1)

    for c in loads[:6]:
        c.wait()
    bases = [
        pltpu.make_async_copy(
            basis_hbm.at[pl.ds(i * (NB * KB // NCHUNK), NB * KB // NCHUNK)],
            basis.at[pl.ds(i * (NB * KB // NCHUNK), NB * KB // NCHUNK)],
            basis_sem.at[i],
        )
        for i in range(NCHUNK)
    ]
    for c in bases:
        c.start()

    row = iota((16, 128), 0)
    lane = iota((16, 128), 1)

    def pack_z(acc, y, vals, from_lane):
        for c, v in enumerate(vals):
            at = 2 * y + c
            acc = jnp.where(lane == at, pltpu.roll(v, (at + 128 - from_lane) % 128, 1), acc)
        return acc

    def first(y, acc):
        mat = material[y]
        lev = level[y]
        smooth = jax.nn.sigmoid(lev)
        sil = (mat == 2).astype(F32)
        permit = jnp.where(mat == 2, metal_permit, jnp.where(mat == 1, 1.0 + design_contrast * smooth, 1.0))
        rat = time_step / permit
        ratio[y] = rat
        silver[y] = sil
        sx, sy, sz = (rat * cot[c, y] for c in range(3))
        p1[3, y] = sx
        p1[4, y] = sz
        p1[5, y] = sy
        ex, ey, ez = p1[0, y], p1[2, y], p1[1, y]
        for t, couple in enumerate(((ey, ez), (sy, sz))):
            for c, v in enumerate(couple):
                xsend[0, t, c, pl.ds(y, 1), :] = v[0:1]
        return pack_z(acc[0], y, (ex, ey), 0), pack_z(acc[1], y, (sx, sy), 0)

    empty = jnp.zeros((16, 128), F32)
    packs = lax.fori_loop(0, 16, first, (empty, empty), unroll=4)
    for t in range(2):
        zsend[0, t] = packs[t]

    pl.semaphore_wait(barrier, 14 + up_far.astype(jnp.int32) + down_far.astype(jnp.int32))
    for i in range(1, 4):
        pl.semaphore_signal(
            ready_sem.at[0], inc=1, device_id={"by": (yy + i) % 4 * 8 + zz}, device_id_type=MESH
        )

    def moves(r, t, field):
        plus = r % 2 == 0
        step = -1 if plus else 1
        edge, halo = (0, 16) if plus else (16, 0)

        def move(src, dst, i, **where):
            return pltpu.make_async_remote_copy(
                src_ref=src,
                dst_ref=dst,
                send_sem=send_sem.at[2 * r + t, i],
                recv_sem=recv_sem.at[2 * r + t, i],
                device_id=where,
                device_id_type=MESH,
            )

        y_out = by > 0 if plus else by < NBY - 1
        y_in = by < NBY - 1 if plus else by > 0
        x_out = bx > 0 if plus else bx < NBX - 1
        x_in = bx < NBX - 1 if plus else bx > 0
        z_out = gz == 1 if plus else gz == 0
        z_in = gz == 0 if plus else gz == 1
        return (
            (y_out, y_in, move(field.at[pl.ds(3 * t, 2), edge], field.at[pl.ds(3 * t, 2), halo], 0, by=by + step)),
            (x_out, x_in, move(xsend.at[r, t], xrecv.at[r, t], 1, bx=bx + step)),
            (z_out, z_in, move(zsend.at[r, t], zrecv.at[r, t], 2, gz=1 - gz)),
        )

    def send(r, t, field):
        for out, _, c in moves(r, t, field):
            pl.when(out)(c.start)

    def receive(r, t, field, first, last):
        for _, into, c in moves(r, t, field)[first:last]:
            pl.when(into)(c.wait_recv)

    def sent(r, t, field):
        for out, _, c in moves(r, t, field):
            pl.when(out)(c.wait_send)

    send(0, 0, p1)
    send(0, 1, p1)

    for c in loads[6:]:
        c.wait()

    def count(y, _):
        flat = y * 2048 + row * 128 + lane
        total = jnp.zeros((16, 128), F32)
        for i in range(8):
            total = total + (flat == source_ref[i]).astype(F32)
        sources[y] = total
        smooth = jax.nn.sigmoid(level[y])
        design = (material[y] == 1).astype(F32)
        factor[y] = -(design * design_contrast * (smooth * (1.0 - smooth))) * (ratio[y] * (1.0 / time_step))
        return 0

    lax.fori_loop(0, 16, count, 0, unroll=4)

    owner_row = owner[...].astype(F32)
    group_row = group[...].astype(F32)
    ri, ci = iota((NB, NB), 0), iota((NB, NB), 1)
    owner_wide = jnp.broadcast_to(owner_row, (NB, NB))
    owner_col = jnp.sum(jnp.where(ri == ci, owner_wide, 0.0), axis=1, keepdims=True)
    group_col = jnp.sum(jnp.where(ri == ci, jnp.broadcast_to(group_row, (NB, NB)), 0.0), axis=1, keepdims=True)
    same = jnp.logical_and(owner_wide == owner_col, ci < ri)
    rank_col = jnp.sum(same.astype(F32), axis=1, keepdims=True)
    target_col = owner_col * 4.0 + rank_col
    block, tile = iota((NB, TILES), 0), iota((NB, TILES), 1)
    id_sum = jnp.zeros((PLANES, 128), F32)
    dest, id_lane = iota((PLANES, TILES), 0), iota((PLANES, TILES), 1)
    targets, groups = [], []
    for f in range(2):
        pick = block == 2 * tile + f
        targets.append(jnp.sum(jnp.where(pick, target_col, 0.0), axis=0, keepdims=True))
        groups.append(jnp.sum(jnp.where(pick, group_col, 0.0), axis=0, keepdims=True))
    slot_row = (4 * (block % PLANES) + 2 * (block // PLANES)).astype(F32)
    for h in range(2):
        for f in range(2):
            place[:, pl.ds((2 * h + f) * TILES, TILES)] = (
                (targets[f] == slot_row + float(h)).astype(F32).astype(BF16)
            )
    first_slot = (4 * dest).astype(F32)
    for s in range(4):
        hit = jnp.zeros((PLANES, TILES), F32)
        for f in range(2):
            hit = hit + jnp.where(targets[f] == first_slot + float(s), groups[f], 0.0)
        id_sum = jnp.where(id_lane == s, jnp.sum(hit, axis=1, keepdims=True), id_sum)
    vsend[pl.ds(2, PLANES, stride=3), 0, :] = id_sum

    def plus_half(r, t, field, old, out):
        nxt = r + 1

        def body(y, acc):
            zf = zrecv[r, t]
            fx, fy, fz = (field[IDX[(c, t)], y] for c in "xyz")
            dyx = field[IDX[("x", t)], y + 1] - fx
            dyz = field[IDX[("z", t)], y + 1] - fz

            def along_x(v, c):
                return jnp.where(row == 15, xrecv[r, t, c, pl.ds(y, 1), :], pltpu.roll(v, 15, 0)) - v

            def along_z(v, c):
                return jnp.where(lane == 127, pltpu.roll(zf, 127 - 2 * y - c, 1), pltpu.roll(v, 127, 1)) - v

            dxy, dxz = along_x(fy, 0), along_x(fz, 1)
            dzx, dzy = along_z(fx, 0), along_z(fy, 1)
            turn = {"x": dyz - dzy, "y": dzx - dxz, "z": dxy - dyx}
            vals = {}
            for c in "xyz":
                vals[c] = old(t, c, y, turn[c])
                out[IDX[(c, t)], y + 1] = vals[c]
            for i, c in enumerate("yz"):
                xsend[nxt, t, i, pl.ds(y, 1), :] = vals[c][15:16]
            return pack_z(acc, y, (vals["x"], vals["y"]), 127)

        receive(r, t, field, 1, 3)
        acc = lax.fori_loop(0, 15, body, empty, unroll=5)
        receive(r, t, field, 0, 1)
        zsend[nxt, t] = body(15, acc)

    def minus_turn(r, t, field, y):
        zf = zrecv[r, t]
        fx, fy, fz = (field[IDX[(c, t)], y + 1] for c in "xyz")
        dyx = fx - field[IDX[("x", t)], y]
        dyz = fz - field[IDX[("z", t)], y]

        def along_x(v, c):
            return v - jnp.where(row == 0, xrecv[r, t, c, pl.ds(y, 1), :], pltpu.roll(v, 1, 0))

        def along_z(v, c):
            return v - jnp.where(lane == 0, pltpu.roll(zf, 128 - 2 * y - c, 1), pltpu.roll(v, 1, 1))

        dxy, dxz = along_x(fy, 0), along_x(fz, 1)
        dzx, dzy = along_z(fx, 0), along_z(fy, 1)
        return {"x": dyz - dzy, "y": dzx - dxz, "z": dxy - dyx}

    def old_first(s, c, y, turn):
        return turn if s else h0[COMP[c], y] - time_step * turn

    def old_second(s, c, y, turn):
        before = m1[IDX[(c, s)], y + 1]
        return before + turn if s else before - time_step * turn

    for t in range(2):
        plus_half(0, t, p1, old_first, m1)
        send(1, t, m1)

    pl.semaphore_wait(ready_sem.at[0], 3)
    for i in range(1, 4):
        pl.semaphore_signal(ready_sem.at[1], inc=1, device_id={"bx": (bx + i) % 4}, device_id_type=MESH)

    def chunk(p):
        return pl.ds(p * 3, 3)

    def mine():
        return pltpu.make_async_copy(vsend.at[chunk(me)], vrecv.at[chunk(me)], own_sem)

    def spread():
        def one(i, _):
            p = (me + i) % PLANES
            pltpu.make_async_remote_copy(
                src_ref=vsend.at[chunk(p)],
                dst_ref=vrecv.at[chunk(me)],
                send_sem=a2a_sem.at[0],
                recv_sem=a2a_sem.at[1],
                device_id={"bx": p // NBY, "by": p % NBY},
                device_id_type=MESH,
            ).start()
            return 0

        mine().start()
        lax.fori_loop(1, PLANES, one, 0, unroll=4)

    def gathered():
        many = pl.ds(0, (PLANES - 1) * 3)
        pltpu.make_async_copy(vrecv.at[many], vrecv.at[many], a2a_sem.at[1]).wait()
        mine().wait()

    def all_sent():
        many = pl.ds(0, (PLANES - 1) * 3)
        pltpu.make_async_copy(vsend.at[many], vsend.at[many], a2a_sem.at[0]).wait()

    def electric_first(y, acc):
        rat, sil = ratio[y], silver[y]
        turn = minus_turn(1, 0, m1, y)
        vals = {}
        for c in "xyz":
            e = p1[IDX[(c, 0)], y]
            cur = sil * (drude_keep * j0[COMP[c], y] + drude_gain * e)
            drive = turn[c] - cur
            j0[COMP[c], y] = cur
            drive1[COMP[c], y] = drive
            new = e + rat * drive
            if c == "z":
                new = new + source_level * source_wave[0] * sources[y]
            vals[c] = new
            p2[IDX[(c, 0)], y] = new
        for i, c in enumerate("yz"):
            xsend[2, 0, i, pl.ds(y, 1), :] = vals[c][0:1]
        return pack_z(acc, y, (vals["x"], vals["y"]), 0)

    def adjoint_first(y, acc):
        rat, sil = ratio[y], silver[y]
        back = minus_turn(1, 1, m1, y)
        total = jnp.zeros((16, 128), F32)
        vals = {}
        for c in "xyz":
            a = cot[COMP[c], y] - drude_gain * (sil * p1[IDX[(c, 1)], y]) - time_step * back[c]
            adj1[COMP[c], y] = a
            vals[c] = rat * a
            p2[IDX[(c, 1)], y] = vals[c]
            total = total + vals[c] * drive1[COMP[c], y]
        part1[y] = total
        for i, c in enumerate("yz"):
            xsend[2, 1, i, pl.ds(y, 1), :] = vals[c][0:1]
        return pack_z(acc, y, (vals["x"], vals["y"]), 0)

    for t, body in enumerate((electric_first, adjoint_first)):
        receive(1, t, m1, 1, 3)
        pack = lax.fori_loop(1, 16, body, empty, unroll=5)
        receive(1, t, m1, 0, 1)
        zsend[2, t] = body(0, pack)
        send(2, t, p2)
    for t in range(2):
        plus_half(2, t, p2, old_second, m2)
        send(3, t, m2)

    def drive_second(y, _):
        sil = silver[y]
        turn = minus_turn(3, 0, m2, y)
        total = part1[y]
        for c in "xyz":
            cur = sil * (drude_keep * j0[COMP[c], y] + drude_gain * p2[IDX[(c, 0)], y])
            drive = turn[c] - cur
            e_out[COMP[c], y] = drive
            total = total + p1[IDX[(c, 1)], y] * drive
        grad[pl.ds(pl.multiple_of(y * 16, 16), 16), :] = factor[y] * total
        return 0

    receive(3, 0, m2, 1, 3)
    lax.fori_loop(1, 16, drive_second, 0, unroll=5)
    receive(3, 0, m2, 0, 1)
    drive_second(0, 0)
    for c in bases:
        c.wait()

    low128 = iota((16, 128), 1) < 64
    r256, l256 = iota((16, 256), 0), iota((16, 256), 1)

    def tiles(i, _):
        start = pl.multiple_of(i * 16, 16)
        even = grad[pl.ds(2 * start, 16, stride=2), :]
        odd = grad[pl.ds(2 * start + 1, 16, stride=2), :]
        lhs = jnp.concatenate([even.astype(BF16), odd.astype(BF16)], axis=1)
        acc = jnp.zeros((16, 256), F32)
        for j in range(8):
            w = basis[pl.ds(pl.multiple_of(i * 2048 + j * 256, 256), 256), :]
            got = lax.dot_general(lhs, w, (((1,), (1,)), ((), ())), preferred_element_type=F32)
            acc = jnp.where(r256 == 2 * j + l256 // 128, got, acc)
        partial[pl.ds(start, 16), :] = jnp.where(row % 2 == 0, acc[:, :128], acc[:, 128:])
        return 0

    lax.fori_loop(0, 8, tiles, 0, unroll=4)

    part = partial[...]
    turned = pltpu.roll(part, 64, 1)
    low = iota((TILES, 128), 1) < 64
    stack = jnp.concatenate(
        [
            jnp.where(low, part, 0.0),
            jnp.where(low, turned, 0.0),
            jnp.where(low, 0.0, turned),
            jnp.where(low, 0.0, part),
        ],
        axis=0,
    )
    hi, lo = split(stack)
    slots = lax.dot_general(place[...], hi, (((1,), (0,)), ((), ())), preferred_element_type=F32)
    slots = slots + lax.dot_general(place[...], lo, (((1,), (0,)), ((), ())), preferred_element_type=F32)
    for p in range(2):
        vsend[pl.ds(p, PLANES, stride=3), 0, :] = slots[p * PLANES : (p + 1) * PLANES]
    pl.semaphore_wait(ready_sem.at[1], 3)
    spread()

    def fields(y, _):
        rat, sil = ratio[y], silver[y]
        back = minus_turn(3, 1, m2, y)
        for c in "xyz":
            new = p2[IDX[(c, 0)], y] + rat * e_out[COMP[c], y]
            if c == "z":
                new = new + source_level * source_wave[1] * sources[y]
            e_out[COMP[c], y] = new
            adj_drive = -drude_keep * (sil * p1[IDX[(c, 1)], y]) - p2[IDX[(c, 1)], y]
            a_out[COMP[c], y] = adj1[COMP[c], y] + drude_gain * (sil * adj_drive) - time_step * back[c]
        return 0

    receive(3, 1, m2, 0, 3)
    lax.fori_loop(0, 16, fields, 0, unroll=4)

    gathered()
    ids = vrecv[pl.ds(2, PLANES, stride=3), 0, :]
    group_lane = iota((PLANES, GRP_DEV), 1).astype(F32)
    hits = jnp.concatenate(
        [
            jnp.concatenate(
                [(ids[:, 2 * p + h : 2 * p + h + 1] == group_lane).astype(F32).astype(BF16) for h in range(2)], axis=1
            )
            for p in range(2)
        ],
        axis=0,
    )
    vals = jnp.concatenate([vrecv[pl.ds(p, PLANES, stride=3), 0, :] for p in range(2)], axis=0)
    hi, lo = split(vals)
    both = lax.dot_general(hi, hits, (((0,), (0,)), ((), ())), preferred_element_type=F32)
    both = both + lax.dot_general(lo, hits, (((0,), (0,)), ((), ())), preferred_element_type=F32)
    coef_out[...] = both[:KB, :GRP_DEV] + both[KB:, GRP_DEV:]
    for r, field in enumerate((p1, m1, p2, m2)):
        for t in range(2):
            sent(r, t, field)
    all_sent()


def deliver(e_ref, a_ref, coef_ref, e_out, a_out, coef_out, sem):
    pairs = ((e_ref, e_out), (a_ref, a_out), (coef_ref, coef_out))
    copies = [pltpu.make_async_copy(s, d, sem.at[i]) for i, (s, d) in enumerate(pairs)]
    for c in copies:
        c.start()
    for c in copies:
        c.wait()


def local(
    electric_start,
    magnetic_start,
    current_start,
    cotangent,
    level_set,
    material,
    source_cell,
    basis,
    block_owner,
    block_group,
):
    field = (3, 16, 16, 128)
    brick = (16, 16, 128)
    anywhere = pl.BlockSpec(memory_space=pltpu.HBM)
    V, D = pltpu.VMEM, pltpu.SemaphoreType.DMA
    results = pl.pallas_call(
        kernel,
        name="adjoint_step",
        out_shape=(
            V(field, F32),
            V(field, F32),
            V((KB, GRP_DEV), F32),
        ),
        in_specs=[pl.BlockSpec(memory_space=pltpu.SMEM)] + [anywhere] * 9,
        out_specs=(pl.BlockSpec(memory_space=pltpu.VMEM),) * 3,
        scratch_shapes=[
            V((6, 17, 16, 128), F32),
            V((6, 17, 16, 128), F32),
            V((6, 17, 16, 128), F32),
            V((6, 17, 16, 128), F32),
            V(field, F32),
            V(field, F32),
            V(field, F32),
            V(brick, F32),
            V(brick, jnp.int32),
            V(brick, F32),
            V(brick, F32),
            V(brick, F32),
            V(brick, F32),
            V(field, F32),
            V(field, F32),
            V(brick, F32),
            V((256, 128), F32),
            V((NB * KB, TILE), BF16),
            V((1, NB), jnp.int32),
            V((1, NB), jnp.int32),
            V((4, 2, 2, 16, 128), F32),
            V((4, 2, 2, 16, 128), F32),
            V((4, 2, 16, 128), F32),
            V((4, 2, 16, 128), F32),
            V((NB, 4 * TILES), BF16),
            V((TILES, 128), F32),
            V((3 * PLANES, 1, 128), F32),
            V((3 * PLANES, 1, 128), F32),
            D((10,)),
            D((NCHUNK,)),
            D((8, 3)),
            D((8, 3)),
            D((2,)),
            D,
            pltpu.SemaphoreType.REGULAR((2,)),
        ],
        compiler_params=pltpu.CompilerParams(
            collective_id=0, has_side_effects=True, vmem_limit_bytes=56000 << 10
        ),
    )(
        source_cell,
        electric_start,
        magnetic_start,
        current_start,
        cotangent,
        level_set,
        material,
        basis.reshape(NB * KB, TILE),
        block_owner.reshape(1, NB),
        block_group.reshape(1, NB),
    )
    return pl.pallas_call(
        deliver,
        name="deliver",
        out_shape=(
            jax.ShapeDtypeStruct(field, F32),
            jax.ShapeDtypeStruct(field, F32),
            jax.ShapeDtypeStruct((KB, GRP_DEV), F32),
        ),
        in_specs=[pl.BlockSpec(memory_space=pltpu.VMEM)] * 3,
        out_specs=(anywhere,) * 3,
        scratch_shapes=[D((3,))],
        compiler_params=pltpu.CompilerParams(vmem_limit_bytes=2 << 20),
    )(*(pltpu.with_memory_space_constraint(x, pltpu.VMEM) for x in results))


def solution(mesh):
    return jax.shard_map(
        local,
        mesh=mesh,
        in_specs=(
            P(None, "by", "bx", "gz"),
            P(None, "by", "bx", "gz"),
            P(None, "by", "bx", "gz"),
            P(None, "by", "bx", "gz"),
            P("by", "bx", "gz"),
            P("by", "bx", "gz"),
            P(("bx", "by", "gz")),
            P(("bx", "by", "gz"), None, None),
            P(("bx", "by", "gz"), None),
            P(("bx", "by", "gz")),
        ),
        out_specs=(
            P(None, "by", "bx", "gz"),
            P(None, "by", "bx", "gz"),
            P(None, ("bx", "by", "gz")),
        ),
        check_vma=False,
    )
```

```python
import jax
import jax.numpy as jnp
from jax import lax
from jax.experimental import pallas as pl
from jax.experimental.pallas import tpu as pltpu
from jax.sharding import PartitionSpec as P

KB = 64
GRP_DEV = 128
NBX = 4
NBY = 32
PLANES = 128
NB = 256
TILES = 128
TILE = 256
NCHUNK = 8

time_step = 0.5
drude_keep = 0.9
drude_gain = 1.0
metal_permit = 3.0
design_contrast = 5.0
source_level = 3.0
source_wave = (1.0, -0.6, 0.8, -0.4)

F32 = jnp.float32
BF16 = jnp.bfloat16
MESH = pl.DeviceIdType.MESH

IDX = {("x", 0): 0, ("z", 0): 1, ("y", 0): 2, ("x", 1): 3, ("z", 1): 4, ("y", 1): 5}
COMP = {"x": 0, "y": 1, "z": 2}


def iota(shape, dim):
    return lax.broadcasted_iota(jnp.int32, shape, dim)


def split(v):
    hi = v.astype(BF16)
    lo = (v - hi.astype(F32)).astype(BF16)
    return hi, lo


def kernel(
    source_ref,
    e0_hbm,
    h0_hbm,
    j0_hbm,
    cot_hbm,
    level_hbm,
    material_hbm,
    basis_hbm,
    owner_hbm,
    group_hbm,
    e_out,
    a_out,
    coef_out,
    p1,
    p2,
    m1,
    m2,
    h0,
    j0,
    cot,
    level,
    material,
    ratio,
    silver,
    factor,
    sources,
    adj1,
    drive1,
    part1,
    grad,
    basis,
    owner,
    group,
    xsend,
    xrecv,
    zsend,
    zrecv,
    place,
    partial,
    vsend,
    vrecv,
    in_sem,
    basis_sem,
    send_sem,
    recv_sem,
    a2a_sem,
    own_sem,
    ready_sem,
):
    bx, by, gz = lax.axis_index("bx"), lax.axis_index("by"), lax.axis_index("gz")
    me = bx * NBY + by
    yy, zz = by // 8, by % 8

    loads = [
        (material_hbm, material),
        (level_hbm, level),
        (cot_hbm, cot),
        (e0_hbm.at[0], p1.at[0, pl.ds(0, 16)]),
        (e0_hbm.at[2], p1.at[1, pl.ds(0, 16)]),
        (e0_hbm.at[1], p1.at[2, pl.ds(0, 16)]),
        (h0_hbm, h0),
        (j0_hbm, j0),
        (owner_hbm, owner),
        (group_hbm, group),
    ]
    loads = [pltpu.make_async_copy(s, d, in_sem.at[i]) for i, (s, d) in enumerate(loads)]
    for c in loads:
        c.start()

    zrow = jnp.zeros((2, 16, 128), F32)
    for ref, at in ((p1, 16), (p2, 16), (m1, 0), (m2, 0)):
        for t in range(2):
            ref[3 * t : 3 * t + 2, at] = zrow
    for r in range(4):
        for t in range(2):
            xrecv[r, t] = zrow
        zrecv[r] = zrow

    barrier = pltpu.get_barrier_semaphore()

    def hail(**where):
        pl.semaphore_signal(barrier, inc=1, device_id=where, device_id_type=MESH)

    for i in range(1, 8):
        hail(by=yy * 8 + (zz + i) % 8)
    for i in range(1, 4):
        hail(by=(yy + i) % 4 * 8 + zz)
        hail(bx=(bx + i) % 4)
    hail(gz=1 - gz)
    up_far = jnp.logical_and(zz == 7, by < NBY - 1)
    down_far = jnp.logical_and(zz == 0, by > 0)

    @pl.when(up_far)
    def _():
        hail(by=by + 1)

    @pl.when(down_far)
    def _():
        hail(by=by - 1)

    for c in loads[:6]:
        c.wait()
    bases = [
        pltpu.make_async_copy(
            basis_hbm.at[pl.ds(i * (NB * KB // NCHUNK), NB * KB // NCHUNK)],
            basis.at[pl.ds(i * (NB * KB // NCHUNK), NB * KB // NCHUNK)],
            basis_sem.at[i],
        )
        for i in range(NCHUNK)
    ]
    for c in bases:
        c.start()

    row = iota((16, 128), 0)
    lane = iota((16, 128), 1)

    def pack_z(acc, y, vals, from_lane):
        for c, v in enumerate(vals):
            at = 2 * y + c
            acc = jnp.where(lane == at, pltpu.roll(v, (at + 128 - from_lane) % 128, 1), acc)
        return acc

    def first(y, acc):
        mat = material[y]
        lev = level[y]
        smooth = jax.nn.sigmoid(lev)
        sil = (mat == 2).astype(F32)
        permit = jnp.where(mat == 2, metal_permit, jnp.where(mat == 1, 1.0 + design_contrast * smooth, 1.0))
        rat = time_step / permit
        ratio[y] = rat
        silver[y] = sil
        sx, sy, sz = (rat * cot[c, y] for c in range(3))
        p1[3, y] = sx
        p1[4, y] = sz
        p1[5, y] = sy
        ex, ey, ez = p1[0, y], p1[2, y], p1[1, y]
        for t, couple in enumerate(((ey, ez), (sy, sz))):
            for c, v in enumerate(couple):
                xsend[0, t, c, pl.ds(y, 1), :] = v[0:1]
        return pack_z(acc[0], y, (ex, ey), 0), pack_z(acc[1], y, (sx, sy), 0)

    empty = jnp.zeros((16, 128), F32)
    packs = lax.fori_loop(0, 16, first, (empty, empty), unroll=4)
    for t in range(2):
        zsend[0, t] = packs[t]

    pl.semaphore_wait(barrier, 14 + up_far.astype(jnp.int32) + down_far.astype(jnp.int32))
    for i in range(1, 4):
        pl.semaphore_signal(
            ready_sem.at[0], inc=1, device_id={"by": (yy + i) % 4 * 8 + zz}, device_id_type=MESH
        )

    def moves(r, t, field):
        plus = r % 2 == 0
        step = -1 if plus else 1
        edge, halo = (0, 16) if plus else (16, 0)

        def move(src, dst, i, **where):
            return pltpu.make_async_remote_copy(
                src_ref=src,
                dst_ref=dst,
                send_sem=send_sem.at[2 * r + t, i],
                recv_sem=recv_sem.at[2 * r + t, i],
                device_id=where,
                device_id_type=MESH,
            )

        y_out = by > 0 if plus else by < NBY - 1
        y_in = by < NBY - 1 if plus else by > 0
        x_out = bx > 0 if plus else bx < NBX - 1
        x_in = bx < NBX - 1 if plus else bx > 0
        z_out = gz == 1 if plus else gz == 0
        z_in = gz == 0 if plus else gz == 1
        return (
            (y_out, y_in, move(field.at[pl.ds(3 * t, 2), edge], field.at[pl.ds(3 * t, 2), halo], 0, by=by + step)),
            (x_out, x_in, move(xsend.at[r, t], xrecv.at[r, t], 1, bx=bx + step)),
            (z_out, z_in, move(zsend.at[r, t], zrecv.at[r, t], 2, gz=1 - gz)),
        )

    def send(r, t, field):
        for out, _, c in moves(r, t, field):
            pl.when(out)(c.start)

    def receive(r, t, field, first, last):
        for _, into, c in moves(r, t, field)[first:last]:
            pl.when(into)(c.wait_recv)

    def sent(r, t, field):
        for out, _, c in moves(r, t, field):
            pl.when(out)(c.wait_send)

    send(0, 0, p1)
    send(0, 1, p1)

    for c in loads[6:]:
        c.wait()

    def count(y, _):
        flat = y * 2048 + row * 128 + lane
        total = jnp.zeros((16, 128), F32)
        for i in range(8):
            total = total + (flat == source_ref[i]).astype(F32)
        sources[y] = total
        smooth = jax.nn.sigmoid(level[y])
        design = (material[y] == 1).astype(F32)
        factor[y] = -(design * design_contrast * (smooth * (1.0 - smooth))) * (ratio[y] * (1.0 / time_step))
        return 0

    lax.fori_loop(0, 16, count, 0, unroll=4)

    owner_row = owner[...].astype(F32)
    group_row = group[...].astype(F32)
    ri, ci = iota((NB, NB), 0), iota((NB, NB), 1)
    owner_wide = jnp.broadcast_to(owner_row, (NB, NB))
    owner_col = jnp.sum(jnp.where(ri == ci, owner_wide, 0.0), axis=1, keepdims=True)
    group_col = jnp.sum(jnp.where(ri == ci, jnp.broadcast_to(group_row, (NB, NB)), 0.0), axis=1, keepdims=True)
    same = jnp.logical_and(owner_wide == owner_col, ci < ri)
    rank_col = jnp.sum(same.astype(F32), axis=1, keepdims=True)
    target_col = owner_col * 4.0 + rank_col
    block, tile = iota((NB, TILES), 0), iota((NB, TILES), 1)
    id_sum = jnp.zeros((PLANES, 128), F32)
    dest, id_lane = iota((PLANES, TILES), 0), iota((PLANES, TILES), 1)
    targets, groups = [], []
    for f in range(2):
        pick = block == 2 * tile + f
        targets.append(jnp.sum(jnp.where(pick, target_col, 0.0), axis=0, keepdims=True))
        groups.append(jnp.sum(jnp.where(pick, group_col, 0.0), axis=0, keepdims=True))
    slot_row = (4 * (block % PLANES) + 2 * (block // PLANES)).astype(F32)
    for h in range(2):
        for f in range(2):
            place[:, pl.ds((2 * h + f) * TILES, TILES)] = (
                (targets[f] == slot_row + float(h)).astype(F32).astype(BF16)
            )
    first_slot = (4 * dest).astype(F32)
    for s in range(4):
        hit = jnp.zeros((PLANES, TILES), F32)
        for f in range(2):
            hit = hit + jnp.where(targets[f] == first_slot + float(s), groups[f], 0.0)
        id_sum = jnp.where(id_lane == s, jnp.sum(hit, axis=1, keepdims=True), id_sum)
    vsend[pl.ds(2, PLANES, stride=3), 0, :] = id_sum

    def plus_half(r, t, field, old, out):
        nxt = r + 1

        def body(y, acc):
            zf = zrecv[r, t]
            fx, fy, fz = (field[IDX[(c, t)], y] for c in "xyz")
            dyx = field[IDX[("x", t)], y + 1] - fx
            dyz = field[IDX[("z", t)], y + 1] - fz

            def along_x(v, c):
                return jnp.where(row == 15, xrecv[r, t, c, pl.ds(y, 1), :], pltpu.roll(v, 15, 0)) - v

            def along_z(v, c):
                return jnp.where(lane == 127, pltpu.roll(zf, 127 - 2 * y - c, 1), pltpu.roll(v, 127, 1)) - v

            dxy, dxz = along_x(fy, 0), along_x(fz, 1)
            dzx, dzy = along_z(fx, 0), along_z(fy, 1)
            turn = {"x": dyz - dzy, "y": dzx - dxz, "z": dxy - dyx}
            vals = {}
            for c in "xyz":
                vals[c] = old(t, c, y, turn[c])
                out[IDX[(c, t)], y + 1] = vals[c]
            for i, c in enumerate("yz"):
                xsend[nxt, t, i, pl.ds(y, 1), :] = vals[c][15:16]
            return pack_z(acc, y, (vals["x"], vals["y"]), 127)

        receive(r, t, field, 1, 3)
        acc = lax.fori_loop(0, 15, body, empty, unroll=5)
        receive(r, t, field, 0, 1)
        zsend[nxt, t] = body(15, acc)

    def minus_turn(r, t, field, y):
        zf = zrecv[r, t]
        fx, fy, fz = (field[IDX[(c, t)], y + 1] for c in "xyz")
        dyx = fx - field[IDX[("x", t)], y]
        dyz = fz - field[IDX[("z", t)], y]

        def along_x(v, c):
            return v - jnp.where(row == 0, xrecv[r, t, c, pl.ds(y, 1), :], pltpu.roll(v, 1, 0))

        def along_z(v, c):
            return v - jnp.where(lane == 0, pltpu.roll(zf, 128 - 2 * y - c, 1), pltpu.roll(v, 1, 1))

        dxy, dxz = along_x(fy, 0), along_x(fz, 1)
        dzx, dzy = along_z(fx, 0), along_z(fy, 1)
        return {"x": dyz - dzy, "y": dzx - dxz, "z": dxy - dyx}

    def old_first(s, c, y, turn):
        return turn if s else h0[COMP[c], y] - time_step * turn

    def old_second(s, c, y, turn):
        before = m1[IDX[(c, s)], y + 1]
        return before + turn if s else before - time_step * turn

    for t in range(2):
        plus_half(0, t, p1, old_first, m1)
        send(1, t, m1)

    pl.semaphore_wait(ready_sem.at[0], 3)
    for i in range(1, 4):
        pl.semaphore_signal(ready_sem.at[1], inc=1, device_id={"bx": (bx + i) % 4}, device_id_type=MESH)

    def chunk(p):
        return pl.ds(p * 3, 3)

    def mine():
        return pltpu.make_async_copy(vsend.at[chunk(me)], vrecv.at[chunk(me)], own_sem)

    def spread():
        def one(i, _):
            p = (me + i) % PLANES
            pltpu.make_async_remote_copy(
                src_ref=vsend.at[chunk(p)],
                dst_ref=vrecv.at[chunk(me)],
                send_sem=a2a_sem.at[0],
                recv_sem=a2a_sem.at[1],
                device_id={"bx": p // NBY, "by": p % NBY},
                device_id_type=MESH,
            ).start()
            return 0

        mine().start()
        lax.fori_loop(1, PLANES, one, 0, unroll=4)

    def gathered():
        many = pl.ds(0, (PLANES - 1) * 3)
        pltpu.make_async_copy(vrecv.at[many], vrecv.at[many], a2a_sem.at[1]).wait()
        mine().wait()

    def all_sent():
        many = pl.ds(0, (PLANES - 1) * 3)
        pltpu.make_async_copy(vsend.at[many], vsend.at[many], a2a_sem.at[0]).wait()

    def electric_first(y, acc):
        rat, sil = ratio[y], silver[y]
        turn = minus_turn(1, 0, m1, y)
        vals = {}
        for c in "xyz":
            e = p1[IDX[(c, 0)], y]
            cur = sil * (drude_keep * j0[COMP[c], y] + drude_gain * e)
            drive = turn[c] - cur
            j0[COMP[c], y] = cur
            drive1[COMP[c], y] = drive
            new = e + rat * drive
            if c == "z":
                new = new + source_level * source_wave[0] * sources[y]
            vals[c] = new
            p2[IDX[(c, 0)], y] = new
        for i, c in enumerate("yz"):
            xsend[2, 0, i, pl.ds(y, 1), :] = vals[c][0:1]
        return pack_z(acc, y, (vals["x"], vals["y"]), 0)

    def adjoint_first(y, acc):
        rat, sil = ratio[y], silver[y]
        back = minus_turn(1, 1, m1, y)
        total = jnp.zeros((16, 128), F32)
        vals = {}
        for c in "xyz":
            a = cot[COMP[c], y] - drude_gain * (sil * p1[IDX[(c, 1)], y]) - time_step * back[c]
            adj1[COMP[c], y] = a
            vals[c] = rat * a
            p2[IDX[(c, 1)], y] = vals[c]
            total = total + vals[c] * drive1[COMP[c], y]
        part1[y] = total
        for i, c in enumerate("yz"):
            xsend[2, 1, i, pl.ds(y, 1), :] = vals[c][0:1]
        return pack_z(acc, y, (vals["x"], vals["y"]), 0)

    for t, body in enumerate((electric_first, adjoint_first)):
        receive(1, t, m1, 1, 3)
        pack = lax.fori_loop(1, 16, body, empty, unroll=5)
        receive(1, t, m1, 0, 1)
        zsend[2, t] = body(0, pack)
        send(2, t, p2)
    for t in range(2):
        plus_half(2, t, p2, old_second, m2)
        send(3, t, m2)

    def drive_second(y, _):
        sil = silver[y]
        turn = minus_turn(3, 0, m2, y)
        total = part1[y]
        for c in "xyz":
            cur = sil * (drude_keep * j0[COMP[c], y] + drude_gain * p2[IDX[(c, 0)], y])
            drive = turn[c] - cur
            e_out[COMP[c], y] = drive
            total = total + p1[IDX[(c, 1)], y] * drive
        grad[pl.ds(pl.multiple_of(y * 16, 16), 16), :] = factor[y] * total
        return 0

    receive(3, 0, m2, 1, 3)
    lax.fori_loop(1, 16, drive_second, 0, unroll=5)
    receive(3, 0, m2, 0, 1)
    drive_second(0, 0)
    for c in bases:
        c.wait()

    low128 = iota((16, 128), 1) < 64
    r256, l256 = iota((16, 256), 0), iota((16, 256), 1)

    def tiles(i, _):
        start = pl.multiple_of(i * 16, 16)
        even = grad[pl.ds(2 * start, 16, stride=2), :]
        odd = grad[pl.ds(2 * start + 1, 16, stride=2), :]
        lhs = jnp.concatenate([even.astype(BF16), odd.astype(BF16)], axis=1)
        acc = jnp.zeros((16, 256), F32)
        for j in range(8):
            w = basis[pl.ds(pl.multiple_of(i * 2048 + j * 256, 256), 256), :]
            got = lax.dot_general(lhs, w, (((1,), (1,)), ((), ())), preferred_element_type=F32)
            acc = jnp.where(r256 == 2 * j + l256 // 128, got, acc)
        partial[pl.ds(start, 16), :] = jnp.where(row % 2 == 0, acc[:, :128], acc[:, 128:])
        return 0

    lax.fori_loop(0, 8, tiles, 0, unroll=8)

    part = partial[...]
    turned = pltpu.roll(part, 64, 1)
    low = iota((TILES, 128), 1) < 64
    stack = jnp.concatenate(
        [
            jnp.where(low, part, 0.0),
            jnp.where(low, turned, 0.0),
            jnp.where(low, 0.0, turned),
            jnp.where(low, 0.0, part),
        ],
        axis=0,
    )
    halves = jnp.concatenate(split(stack), axis=1)
    slots = lax.dot_general(place[...], halves, (((1,), (0,)), ((), ())), preferred_element_type=F32)
    slots = slots[:, :128] + slots[:, 128:]
    for p in range(2):
        vsend[pl.ds(p, PLANES, stride=3), 0, :] = slots[p * PLANES : (p + 1) * PLANES]
    pl.semaphore_wait(ready_sem.at[1], 3)
    spread()

    def fields(y, _):
        rat, sil = ratio[y], silver[y]
        back = minus_turn(3, 1, m2, y)
        for c in "xyz":
            new = p2[IDX[(c, 0)], y] + rat * e_out[COMP[c], y]
            if c == "z":
                new = new + source_level * source_wave[1] * sources[y]
            e_out[COMP[c], y] = new
            adj_drive = -drude_keep * (sil * p1[IDX[(c, 1)], y]) - p2[IDX[(c, 1)], y]
            a_out[COMP[c], y] = adj1[COMP[c], y] + drude_gain * (sil * adj_drive) - time_step * back[c]
        return 0

    receive(3, 1, m2, 0, 3)
    lax.fori_loop(0, 16, fields, 0, unroll=4)

    gathered()
    ids = vrecv[pl.ds(2, PLANES, stride=3), 0, :]
    group_lane = iota((PLANES, GRP_DEV), 1).astype(F32)
    hits = jnp.concatenate(
        [
            jnp.concatenate(
                [(ids[:, 2 * p + h : 2 * p + h + 1] == group_lane).astype(F32).astype(BF16) for h in range(2)], axis=1
            )
            for p in range(2)
        ],
        axis=0,
    )
    vals = jnp.concatenate([vrecv[pl.ds(p, PLANES, stride=3), 0, :] for p in range(2)], axis=0)
    hi, lo = split(vals)
    both = lax.dot_general(hi, hits, (((0,), (0,)), ((), ())), preferred_element_type=F32)
    both = both + lax.dot_general(lo, hits, (((0,), (0,)), ((), ())), preferred_element_type=F32)
    coef_out[...] = both[:KB, :GRP_DEV] + both[KB:, GRP_DEV:]
    for r, field in enumerate((p1, m1, p2, m2)):
        for t in range(2):
            sent(r, t, field)
    all_sent()


def deliver(e_ref, a_ref, coef_ref, e_out, a_out, coef_out, sem):
    pairs = ((e_ref, e_out), (a_ref, a_out), (coef_ref, coef_out))
    copies = [pltpu.make_async_copy(s, d, sem.at[i]) for i, (s, d) in enumerate(pairs)]
    for c in copies:
        c.start()
    for c in copies:
        c.wait()


def local(
    electric_start,
    magnetic_start,
    current_start,
    cotangent,
    level_set,
    material,
    source_cell,
    basis,
    block_owner,
    block_group,
):
    field = (3, 16, 16, 128)
    brick = (16, 16, 128)
    anywhere = pl.BlockSpec(memory_space=pltpu.HBM)
    V, D = pltpu.VMEM, pltpu.SemaphoreType.DMA
    results = pl.pallas_call(
        kernel,
        name="adjoint_step",
        out_shape=(
            V(field, F32),
            V(field, F32),
            V((KB, GRP_DEV), F32),
        ),
        in_specs=[pl.BlockSpec(memory_space=pltpu.SMEM)] + [anywhere] * 9,
        out_specs=(pl.BlockSpec(memory_space=pltpu.VMEM),) * 3,
        scratch_shapes=[
            V((6, 17, 16, 128), F32),
            V((6, 17, 16, 128), F32),
            V((6, 17, 16, 128), F32),
            V((6, 17, 16, 128), F32),
            V(field, F32),
            V(field, F32),
            V(field, F32),
            V(brick, F32),
            V(brick, jnp.int32),
            V(brick, F32),
            V(brick, F32),
            V(brick, F32),
            V(brick, F32),
            V(field, F32),
            V(field, F32),
            V(brick, F32),
            V((256, 128), F32),
            V((NB * KB, TILE), BF16),
            V((1, NB), jnp.int32),
            V((1, NB), jnp.int32),
            V((4, 2, 2, 16, 128), F32),
            V((4, 2, 2, 16, 128), F32),
            V((4, 2, 16, 128), F32),
            V((4, 2, 16, 128), F32),
            V((NB, 4 * TILES), BF16),
            V((TILES, 128), F32),
            V((3 * PLANES, 1, 128), F32),
            V((3 * PLANES, 1, 128), F32),
            D((10,)),
            D((NCHUNK,)),
            D((8, 3)),
            D((8, 3)),
            D((2,)),
            D,
            pltpu.SemaphoreType.REGULAR((2,)),
        ],
        compiler_params=pltpu.CompilerParams(
            collective_id=0, has_side_effects=True, vmem_limit_bytes=56000 << 10
        ),
    )(
        source_cell,
        electric_start,
        magnetic_start,
        current_start,
        cotangent,
        level_set,
        material,
        basis.reshape(NB * KB, TILE),
        block_owner.reshape(1, NB),
        block_group.reshape(1, NB),
    )
    return pl.pallas_call(
        deliver,
        name="deliver",
        out_shape=(
            jax.ShapeDtypeStruct(field, F32),
            jax.ShapeDtypeStruct(field, F32),
            jax.ShapeDtypeStruct((KB, GRP_DEV), F32),
        ),
        in_specs=[pl.BlockSpec(memory_space=pltpu.VMEM)] * 3,
        out_specs=(anywhere,) * 3,
        scratch_shapes=[D((3,))],
        compiler_params=pltpu.CompilerParams(vmem_limit_bytes=2 << 20),
    )(*(pltpu.with_memory_space_constraint(x, pltpu.VMEM) for x in results))


def solution(mesh):
    return jax.shard_map(
        local,
        mesh=mesh,
        in_specs=(
            P(None, "by", "bx", "gz"),
            P(None, "by", "bx", "gz"),
            P(None, "by", "bx", "gz"),
            P(None, "by", "bx", "gz"),
            P("by", "bx", "gz"),
            P("by", "bx", "gz"),
            P(("bx", "by", "gz")),
            P(("bx", "by", "gz"), None, None),
            P(("bx", "by", "gz"), None),
            P(("bx", "by", "gz")),
        ),
        out_specs=(
            P(None, "by", "bx", "gz"),
            P(None, "by", "bx", "gz"),
            P(None, ("bx", "by", "gz")),
        ),
        check_vma=False,
    )
```
